512 devices in a mesh: lat: 64 (over z_lo, x, core), wid: 8 (over z_hi, y).
Axes of the slice: x: 4, y: 4, z: 16 (z_hi: 2, z_lo: 8; z = z_hi * 8 + z_lo), core: 2. Of those that a mesh axis runs over, the one named last changes fastest.
Arguments:
- activations: bfloat16 [8192, 4096], P('lat', 'wid'), may hold values from -1.1953125 to 1.1953125
- block_ids: int32 [8192, 4], P('lat'), may hold values from 0 to 511, all different within a row; in each aligned block of 128 rows (0 to 127, 128 to 255, ...) at most 2 rows name the same one
- alive_tallies: int32 [8192], P('lat'), may hold values from 2 to 4
- encoder: bfloat16 [4096, 65536], P('wid', 'lat'), may hold values from -0.5 to 0.5
- encoder_bias: float32 [65536], P('lat'), may hold values from -3 to 3
- decoder: bfloat16 [65536, 4096], P('lat', 'wid'), may hold values from -3.2 to 3.2
Outputs:
- encoder_grad: bfloat16 [4096, 65536], P('wid', 'lat')
- decoder_grad: bfloat16 [65536, 4096], P('lat', 'wid')
- bias_grad: float32 [65536], P('lat')
The draws below stay inside these ranges and needn't reach their ends.
Inputs may be any that keep to these rules, and one draw needn't show every extreme that they name: `block_ids`: the 4 ids of a row are distinct. Among the 128 rows of one index of lat no id stands more than 2 times, and some id stands exactly 2 times.
All inputs are finite; a program needn't handle non-finite values.
Results may differ from the reference program's by a relative error of at most 0.009.
Values may be sent and summed in bfloat16 or wider, within the bound.
A program may use at most 64 MiB of HBM per device.

```python
import math
import jax
import jax.numpy as jnp
import numpy as np
from jax import lax

D = 4096
BS = 128
LIVE_PLACES = 4
ROWS_DEV = 128
HIDDEN_GROUPS = 512
LATENTS = 65536
ROWS = 8192
CAP = 2
N_LAT = 64


def draw_decoder(key, part):
    key_rows, key_cols, key_base = jax.random.split(key, 3)
    row_scale = jnp.exp(jax.random.uniform(key_rows, (LATENTS, 1), jnp.float32) * math.log(10.0))
    ramp = jnp.exp(jnp.arange(D, dtype=jnp.float32)[None, :] / D * math.log(3.0))
    col_scale = jnp.exp(jax.random.uniform(key_cols, (1, D), jnp.float32) * math.log(10.0)) * ramp
    base = jnp.clip(jax.random.normal(key_base, (LATENTS, D), jnp.float32), -6.0, 6.0)
    return (base * row_scale * col_scale / 576.0).astype(jnp.bfloat16)


def set_ends(result, rng, low, top_value):
    spot = [jax.random.randint(jax.random.fold_in(rng, axis), (), 0, length) for axis, length in enumerate(result.shape)]
    widest = result.shape.index(max(result.shape))
    neighbour = spot[:widest] + [(spot[widest] + 1) % result.shape[widest]] + spot[widest + 1:]
    return result.at[tuple(spot)].set(low).at[tuple(neighbour)].set(top_value)


def steps_of(rng, shape, cuts, smallest, high):
    loudness = 1.0
    for dim, shards_of in cuts:
        steps = jax.random.uniform(jax.random.fold_in(jax.random.fold_in(rng, 6), dim), (shards_of,), jnp.float32, smallest / len(cuts), high / len(cuts))
        loudness = loudness * jnp.repeat(jnp.exp(steps), shape[dim] // shards_of).reshape((-1,) + (1,) * (len(shape) - 1 - dim))
    return loudness


def routed_block(rng, own, number, rows, count, top, reach, skew):
    ranking = jax.random.permutation(rng, count)
    packed, usual = load_shares(count, rows * top, reach, skew, True), load_shares(count, rows * top, reach, skew, False)
    places = jnp.arange(count)

    def named(tallies, offset_by):
        used = int((tallies > 0).sum())
        fixed = max(1, used // 4)
        passed = fixed + (places - fixed + offset_by * (used - fixed)) % max(1, count - fixed)
        return jnp.zeros((count,), jnp.int32).at[ranking[jnp.where(places < fixed, places, passed)]].set(jnp.asarray(tallies, jnp.int32))

    tallies = jnp.where(number % 4 == 0, named(packed, number // 4), named(usual, number - number // 4 - 1))
    mixed = jax.random.permutation(jax.random.fold_in(own, 3), count)
    source_of, taker = mixed[0:count // 2 * 2:2], mixed[1:count // 2 * 2:2]
    slack = jnp.minimum(tallies[source_of] - 1, reach - tallies[taker]) // 2
    slack = jnp.where((source_of == ranking[0]) | (taker == ranking[0]) | (tallies[taker] == 0), 0, jnp.maximum(slack, 0))
    passed = jax.random.randint(jax.random.fold_in(own, 4), (count // 2,), 0, 1 << 20) % (slack + 1)
    tallies = tallies.at[source_of].add(-passed).at[taker].add(passed)
    items = jnp.searchsorted(jnp.cumsum(tallies), jnp.arange(rows * top), side="right").astype(jnp.int32)
    table = items.reshape(top, rows).T
    table = table[jax.random.permutation(jax.random.fold_in(own, 1), rows)]
    offset_by = jax.random.randint(jax.random.fold_in(own, 2), (rows, 1), 0, top)
    return jnp.take_along_axis(table, (jnp.arange(top)[None, :] + offset_by) % top, axis=1)


def load_shares(number_of, total, bound, skew, full):
    portions = [(1 << 20) // math.isqrt(rank ** skew) + 1 for rank in range(1, number_of + 1)]
    largest = bound if full else min(bound, max(-(-total // number_of), total * portions[0] // sum(portions)))
    least = 1 if total - largest >= number_of - 1 else 0
    holding, surplus = [largest] + [least] * (number_of - 1), total - largest - least * (number_of - 1)
    while surplus > 0:
        movable = [i for i in range(1, number_of) if holding[i] < largest] or [i for i in range(1, number_of) if holding[i] < bound]
        mass, left = sum([portions[i] for i in movable]), surplus
        for i in movable:
            more = min(bound - holding[i], max(1, left * portions[i] // mass), surplus)
            holding[i] = holding[i] + more
            surplus = surplus - more
    return np.array(holding)


def gaussian(rng, dims, deviation, reach, cuts=(), kind=jnp.bfloat16):
    values = deviation * jax.random.normal(rng, dims, jnp.float32)
    if cuts:
        values = values * steps_of(rng, dims, cuts, -0.22, 0.18)
    return jnp.clip(values, -reach, reach).astype(kind)


def setup_inputs(seed: int = 0) -> dict:
    keys = jax.random.split(jax.random.key(seed), 7)
    activations = gaussian(keys[0], (ROWS, D), 0.2, 1.1953125, ((0, 64), (1, 8)))
    block_ids_keys = jax.random.split(jax.random.fold_in(keys[1], 1), ROWS // ROWS_DEV)
    block_ids_turns = jax.random.permutation(jax.random.fold_in(keys[1], 3), ROWS // ROWS_DEV)
    block_ids = jax.vmap(lambda own, number: routed_block(jax.random.fold_in(keys[1], 2), own, number, ROWS_DEV, HIDDEN_GROUPS, LIVE_PLACES, CAP, 2))(block_ids_keys, block_ids_turns).reshape((ROWS, LIVE_PLACES))
    alive_tallies = set_ends(jax.random.randint(keys[2], (ROWS,), LIVE_PLACES // 2, LIVE_PLACES + 1), jax.random.fold_in(keys[2], 1), LIVE_PLACES // 2, LIVE_PLACES).astype(jnp.int32)
    encoder = gaussian(keys[3], (D, LATENTS), (D // 25) ** -0.5, 0.5, ((0, 8), (1, 64)))
    encoder_bias = gaussian(keys[4], (LATENTS,), 0.5, 3.0, ((0, 64),), jnp.float32)
    decoder = draw_decoder(jax.random.fold_in(keys[6], 71), 0)
    return dict(activations=activations, block_ids=block_ids, alive_tallies=alive_tallies, encoder=encoder, encoder_bias=encoder_bias, decoder=decoder)


epsilon = 1e-06

def activate(values):
    return jax.nn.gelu(values, approximate=True)

def slot_ranks(blocks_flat):
    slot_total = blocks_flat.shape[0]
    slot_order = jnp.arange(slot_total, dtype=jnp.int32)
    earlier = (blocks_flat[:, None] == blocks_flat[None, :]) & (slot_order[:, None] > slot_order[None, :])
    return lax.optimization_barrier(jnp.sum(earlier.astype(jnp.int32), axis=1)).astype(jnp.int32)

def reference(activations, block_ids, alive_tallies, encoder, encoder_bias, decoder):
    place_number = ROWS_DEV * LIVE_PLACES
    layer_height = N_LAT * CAP
    filler_position = ROWS * LIVE_PLACES
    shard_groups = block_ids.reshape(N_LAT, place_number)
    ranks = lax.map(slot_ranks, shard_groups)
    group_alive_flags = (jnp.arange(LIVE_PLACES, dtype=jnp.int32)[None, :] < alive_tallies[:, None]).reshape(N_LAT, place_number)
    device_index = jnp.arange(N_LAT, dtype=jnp.int32)[:, None]
    entry_position = (device_index * CAP + ranks).astype(jnp.int32)
    place_label = (device_index * place_number + jnp.arange(place_number, dtype=jnp.int32)[None, :]).astype(jnp.int32)
    mapping_array = jnp.full((HIDDEN_GROUPS, layer_height), filler_position, jnp.int32).at[shard_groups, entry_position].set(jnp.where(group_alive_flags, place_label, filler_position).astype(jnp.int32))
    padded_rows = jnp.concatenate([activations, jnp.zeros((1, D), jnp.bfloat16)], axis=0)
    row_sq = lax.optimization_barrier(jnp.sum(jnp.square(decoder.astype(jnp.float32)), axis=1))
    row_norm = jnp.sqrt(row_sq + epsilon)
    unit_rows = (decoder.astype(jnp.float32) / row_norm[:, None]).astype(jnp.bfloat16)

    def forward_block(recon, block_index):
        slot_ids = mapping_array[block_index]
        rows = (slot_ids // LIVE_PLACES).astype(jnp.int32)
        live = (slot_ids < filler_position).astype(jnp.float32)[:, None]
        gathered = padded_rows[rows]
        start = (block_index * BS).astype(jnp.int32)
        weights = lax.dynamic_slice_in_dim(encoder, start, BS, 1)
        bias = lax.dynamic_slice_in_dim(encoder_bias, start, BS, 0)
        preact = jnp.dot(gathered, weights, preferred_element_type=jnp.float32) + bias[None, :]
        latent_codes = (activate(preact) * live).astype(jnp.bfloat16)
        unit_block = lax.dynamic_slice_in_dim(unit_rows, start, BS, 0)
        term = jnp.dot(latent_codes, unit_block, preferred_element_type=jnp.float32).astype(jnp.bfloat16)
        recon = recon.at[rows].add(term.astype(jnp.float32))
        return (recon, (preact, latent_codes))
    recon, (preacts, codes_all) = lax.scan(forward_block, jnp.zeros((ROWS + 1, D), jnp.float32), jnp.arange(HIDDEN_GROUPS, dtype=jnp.int32))
    residual = (recon[:ROWS] - activations.astype(jnp.float32)).astype(jnp.bfloat16)
    padded_resid = jnp.concatenate([residual, jnp.zeros((1, D), jnp.bfloat16)], axis=0)

    def backward_block(inputs):
        block_index, preact, latent_codes = inputs
        slot_ids = mapping_array[block_index]
        rows = (slot_ids // LIVE_PLACES).astype(jnp.int32)
        live = (slot_ids < filler_position).astype(jnp.float32)[:, None]
        gathered = padded_rows[rows]
        resid = padded_resid[rows]
        start = (block_index * BS).astype(jnp.int32)
        unit_block = lax.dynamic_slice_in_dim(unit_rows, start, BS, 0)
        norm_block = lax.dynamic_slice_in_dim(row_norm, start, BS, 0)
        dcode = jnp.dot(resid, unit_block.T, preferred_element_type=jnp.float32)
        gated, pullback = jax.vjp(activate, preact)
        dpre = pullback(dcode)[0] * live
        half_preact_gradient = dpre.astype(jnp.bfloat16)
        enc_block = jnp.dot(gathered.T, half_preact_gradient, preferred_element_type=jnp.float32).astype(jnp.bfloat16)
        raw = jnp.dot(latent_codes.T, resid, preferred_element_type=jnp.float32)
        unit_wide = unit_block.astype(jnp.float32)
        along = lax.optimization_barrier(jnp.sum(raw * unit_wide, axis=1))
        dec_block = ((raw - along[:, None] * unit_wide) / norm_block[:, None]).astype(jnp.bfloat16)
        return (enc_block, dec_block, lax.optimization_barrier(jnp.sum(dpre, axis=0)))
    encoder_blocks, dec_blocks, bias_blocks = lax.map(backward_block, (jnp.arange(HIDDEN_GROUPS, dtype=jnp.int32), preacts, codes_all))
    encoder_grad = jnp.transpose(encoder_blocks, (1, 0, 2)).reshape(D, HIDDEN_GROUPS * BS)
    decoder_grad = dec_blocks.reshape(HIDDEN_GROUPS * BS, D)
    bias_grad = bias_blocks.reshape(HIDDEN_GROUPS * BS)
    return (encoder_grad, decoder_grad, bias_grad)
```

```python
import functools

import jax
import jax.numpy as jnp
from jax import lax
from jax.experimental import pallas as pl
from jax.experimental.pallas import tpu as pltpu
from jax.sharding import PartitionSpec as P

BS = 128
EPS = 1e-06
C0 = 0.7978845608
C1 = 0.044715
FILLER = 2.0
MESH = pl.DeviceIdType.MESH


def gelu(v):
    return 0.5 * v * (1.0 + jnp.tanh(C0 * (v + C1 * v * v * v)))


def gelu_slope(v):
    t = jnp.tanh(C0 * (v + C1 * v * v * v))
    return 0.5 * (1.0 + t) + 0.5 * v * (1.0 - t * t) * C0 * (1.0 + 3.0 * C1 * v * v)


def wid_place():
    me = lax.axis_index("wid")
    hi, y = me // 4, me % 4
    partner = (1 - hi) * 4 + y
    peers = [hi * 4 + (y + d) % 4 for d in (1, 2, 3)]
    return hi, y, partner, peers


def greet(others):
    barrier = pltpu.get_barrier_semaphore()
    for other in others:
        pl.semaphore_signal(barrier, inc=1, device_id={"wid": other}, device_id_type=MESH)
    pl.semaphore_wait(barrier, len(others))


def send(src, dst, send_sem, recv_sem, to):
    copy = pltpu.make_async_remote_copy(
        src_ref=src,
        dst_ref=dst,
        send_sem=send_sem,
        recv_sem=recv_sem,
        device_id={"wid": to},
        device_id_type=MESH,
    )
    copy.start()
    return copy


def scatter_sums(part_ref, got_y, mine, got_z, sems, place):
    hi, y, partner, peers = place
    copies = [
        send(part_ref.at[:, (y + d) % 4], got_y.at[d - 1], sems.at[0, d - 1], sems.at[1, d - 1], peers[d - 1])
        for d in (1, 2, 3)
    ]
    for copy in copies:
        copy.wait()

    def total(h):
        s = part_ref[h, y].astype(jnp.float32)
        for d in range(3):
            s = s + got_y[d, h].astype(jnp.float32)
        return s

    mine[...] = total(1 - hi).astype(mine.dtype)
    copy = send(mine, got_z, sems.at[0, 3], sems.at[1, 3], partner)
    own = total(hi)
    copy.wait()
    return own + got_z[...].astype(jnp.float32)


def gather_start(out_ref, sems, base, place):
    hi, y, partner, peers = place
    block = out_ref.at[hi, y]
    far = send(block, block, sems.at[0, base], sems.at[1, base], partner)
    near = [
        send(block, block, sems.at[0, base + d], sems.at[1, base + d], peers[d - 1]) for d in (1, 2, 3)
    ]
    return far, near


def gather_pass(out_ref, sems, base, far, place):
    hi, y, partner, peers = place
    far.wait()
    block = out_ref.at[1 - hi, y]
    return [
        send(block, block, sems.at[0, base + 3 + d], sems.at[1, base + 3 + d], peers[d - 1])
        for d in (1, 2, 3)
    ]


def forward_kernel(part_ref, sq_ref, bias_ref, live_ref, codes_ref, pre_ref, own_ref, row_ref,
                   got_y, mine, got_z, sq_y, sq_mine, sq_z, sems):
    place = wid_place()
    hi, y, partner, peers = place
    greet([partner] + peers)
    sq_copies = [
        send(sq_ref, sq_y.at[d - 1], sems.at[0, 10 + d], sems.at[1, 10 + d], peers[d - 1]) for d in (1, 2, 3)
    ]
    for copy in sq_copies:
        copy.wait()
    sq_mine[...] = sq_ref[...] + sq_y[0] + sq_y[1] + sq_y[2]
    sq_far = send(sq_mine, sq_z, sems.at[0, 14], sems.at[1, 14], partner)
    preact = scatter_sums(part_ref, got_y, mine, got_z, sems, place) + bias_ref[...]
    pre_ref[...] = preact
    codes = (gelu(preact) * live_ref[...]).astype(jnp.bfloat16)
    own_ref[...] = codes
    codes_ref[hi, y] = codes
    far, near = gather_start(codes_ref, sems, 4, place)
    sq_far.wait()
    row_ref[...] = sq_mine[...] + sq_z[...]
    late = gather_pass(codes_ref, sems, 4, far, place)
    for copy in near + late:
        copy.wait()


def backward_kernel(part_ref, pre_ref, own_ref, live_ref, dpre_ref, small_ref, got_y, mine, got_z, sems):
    place = wid_place()
    hi, y, partner, peers = place
    greet([partner] + peers)
    dcode = scatter_sums(part_ref, got_y, mine, got_z, sems, place)
    dpre = dcode * gelu_slope(pre_ref[...]) * live_ref[...]
    dpre_ref[hi, y] = dpre.astype(jnp.bfloat16)
    far, near = gather_start(dpre_ref, sems, 4, place)
    along = jnp.sum(own_ref[...].astype(jnp.float32) * dcode, axis=0, keepdims=True)
    bias_grad = jnp.sum(dpre, axis=0, keepdims=True)
    row = lax.broadcasted_iota(jnp.int32, (8, BS), 0)
    small_ref[hi, y] = jnp.where(row == 0, along, bias_grad)
    small_far, small_near = gather_start(small_ref, sems, 11, place)
    late = gather_pass(dpre_ref, sems, 4, far, place)
    small_late = gather_pass(small_ref, sems, 11, small_far, place)
    for copy in near + late + small_near + small_late:
        copy.wait()


def vmem(n):
    return [pl.BlockSpec(memory_space=pltpu.VMEM)] * n


def sum_scratch(slots):
    return [
        pltpu.VMEM((3, 2, slots, BS), jnp.bfloat16),
        pltpu.VMEM((slots, BS), jnp.bfloat16),
        pltpu.VMEM((slots, BS), jnp.bfloat16),
    ]


def forward_sums(part, sq, bias, live):
    slots = part.shape[2]
    return pl.pallas_call(
        forward_kernel,
        out_shape=(
            jax.ShapeDtypeStruct((2, 4, slots, BS), jnp.bfloat16),
            jax.ShapeDtypeStruct((slots, BS), jnp.float32),
            jax.ShapeDtypeStruct((slots, BS), jnp.bfloat16),
            jax.ShapeDtypeStruct((8, BS), jnp.float32),
        ),
        in_specs=vmem(4),
        out_specs=tuple(vmem(4)),
        scratch_shapes=sum_scratch(slots)
        + [
            pltpu.VMEM((3, 8, BS), jnp.float32),
            pltpu.VMEM((8, BS), jnp.float32),
            pltpu.VMEM((8, BS), jnp.float32),
            pltpu.SemaphoreType.DMA((2, 15)),
        ],
        compiler_params=pltpu.CompilerParams(collective_id=0, has_side_effects=True),
        name="forward_sums",
    )(part, sq, bias, live)


def backward_sums(part, pre, own, live):
    slots = part.shape[2]
    return pl.pallas_call(
        backward_kernel,
        out_shape=(
            jax.ShapeDtypeStruct((2, 4, slots, BS), jnp.bfloat16),
            jax.ShapeDtypeStruct((2, 4, 8, BS), jnp.float32),
        ),
        in_specs=vmem(4),
        out_specs=tuple(vmem(2)),
        scratch_shapes=sum_scratch(slots) + [pltpu.SemaphoreType.DMA((2, 18))],
        compiler_params=pltpu.CompilerParams(collective_id=1, has_side_effects=True),
        name="backward_sums",
    )(part, pre, own, live)


def to_owner(x, lat):
    features = x.shape[-1]
    x = lax.all_to_all(x.reshape(lat, 16, features), "lat", split_axis=0, concat_axis=0, tiled=True)
    return x.reshape(lat, 8, 2, features).transpose(1, 0, 2, 3).reshape(8, lat * 2, features)


def to_row(x, lat):
    features = x.shape[-1]
    x = x.reshape(8, lat, 2, features).transpose(1, 0, 2, 3).reshape(lat, 16, features)
    x = lax.all_to_all(x, "lat", split_axis=0, concat_axis=0, tiled=True)
    return x.reshape(lat * 16, features)


def body(activations, block_ids, alive_tallies, encoder, encoder_bias, decoder):
    rows, features = activations.shape
    slots = block_ids.shape[1]
    lat = lax.axis_size("lat")
    wid = lax.axis_index("wid")
    positions = lat * 16
    f32 = jnp.float32

    flat = block_ids.reshape(rows * slots)
    order = jnp.arange(rows * slots, dtype=jnp.int32)
    earlier = (flat[:, None] == flat[None, :]) & (order[None, :] < order[:, None])
    rank = jnp.sum(earlier.astype(jnp.int32), axis=1).reshape(rows, slots)
    alive = jnp.arange(slots, dtype=jnp.int32)[None, :] < alive_tallies[:, None]
    position = jnp.where(alive, block_ids * 2 + rank, -1)
    spots = jnp.arange(positions, dtype=jnp.int32)[:, None]
    place = spots == position[:, 0][None, :]
    for j in range(1, slots):
        place = place | (spots == position[:, j][None, :])
    filled = jnp.any(place, axis=1, keepdims=True)
    place = place.astype(jnp.bfloat16)

    outgoing = jnp.dot(place, activations, preferred_element_type=f32)
    outgoing = jnp.where(filled, outgoing, FILLER).astype(jnp.bfloat16)
    incoming = to_owner(outgoing, lat)
    live = (incoming[:, :, 0] < 1.5).astype(f32)
    own_live = jnp.broadcast_to(
        lax.dynamic_index_in_dim(live, wid, 0, keepdims=False)[:, None], (lat * 2, BS)
    )

    decoder_wide = decoder.astype(f32)
    local_sq = jnp.sum(jnp.square(decoder_wide), axis=1).reshape(8, BS)
    encoder_blocks = encoder.reshape(features, 8, BS)
    partial_pre = jnp.einsum(
        "aec,caw->aew", incoming, encoder_blocks, preferred_element_type=f32
    ).astype(jnp.bfloat16)
    own_bias = lax.dynamic_index_in_dim(encoder_bias.reshape(8, BS), wid, 0, keepdims=True)
    codes, own_pre, own_codes, row_sq = forward_sums(
        partial_pre.reshape(2, 4, lat * 2, BS), local_sq, own_bias, own_live
    )
    codes = codes.reshape(8, lat * 2, BS)
    row_norm = jnp.sqrt(row_sq + EPS)[:, :, None]
    unit = (decoder_wide.reshape(8, BS, features) / row_norm).astype(jnp.bfloat16)

    terms = jnp.einsum("jkr,jrs->jks", codes, unit, preferred_element_type=f32).astype(jnp.bfloat16)
    returned = to_row(terms, lat)
    recon = lax.dot_general(place, returned, (((0,), (0,)), ((), ())), preferred_element_type=f32)
    residual = (recon - activations.astype(f32)).astype(jnp.bfloat16)
    resid_send = jnp.dot(place, residual, preferred_element_type=f32).astype(jnp.bfloat16)
    resid_in = to_owner(resid_send, lat)

    partial_dcode = jnp.einsum(
        "zea,zxa->zex", resid_in, unit, preferred_element_type=f32
    ).astype(jnp.bfloat16)
    dpre, small = backward_sums(
        partial_dcode.reshape(2, 4, lat * 2, BS), own_pre, own_codes, own_live
    )
    dpre = dpre.reshape(8, lat * 2, BS)
    small = small.reshape(8, 8, BS)
    raw = jnp.einsum("ekc,ekv->ecv", codes, resid_in, preferred_element_type=f32)
    along = small[:, 0, :, None]
    bias_grad = small[:, 1].reshape(8 * BS)
    encoder_grad = (
        jnp.einsum("kiy,kif->ykf", incoming, dpre, preferred_element_type=f32)
        .reshape(features, 8 * BS)
        .astype(jnp.bfloat16)
    )
    decoder_grad = (
        ((raw - along * unit.astype(f32)) / row_norm).astype(jnp.bfloat16).reshape(8 * BS, features)
    )
    return encoder_grad, decoder_grad, bias_grad


def solution(mesh):
    return jax.shard_map(
        body,
        mesh=mesh,
        in_specs=(
            P("lat", "wid"),
            P("lat", None),
            P("lat"),
            P("wid", "lat"),
            P("lat"),
            P("lat", "wid"),
        ),
        out_specs=(P("wid", "lat"), P("lat", "wid"), P("lat")),
        check_vma=False,
    )
```

```python
import functools

import jax
import jax.numpy as jnp
from jax import lax
from jax.experimental import pallas as pl
from jax.experimental.pallas import tpu as pltpu
from jax.sharding import PartitionSpec as P

BS = 128
EPS = 1e-06
C0 = 0.7978845608
C1 = 0.044715
FILLER = 2.0
LINE = 8
PLANE = 8
MESH = pl.DeviceIdType.MESH


def gelu(v):
    return 0.5 * v * (1.0 + jnp.tanh(C0 * (v + C1 * v * v * v)))


def gelu_slope(v):
    t = jnp.tanh(C0 * (v + C1 * v * v * v))
    return 0.5 * (1.0 + t) + 0.5 * v * (1.0 - t * t) * C0 * (1.0 + 3.0 * C1 * v * v)


def wid_place():
    me = lax.axis_index("wid")
    hi, y = me // 4, me % 4
    partner = (1 - hi) * 4 + y
    peers = [hi * 4 + (y + d) % 4 for d in (1, 2, 3)]
    return hi, y, partner, peers


def greet(others):
    barrier = pltpu.get_barrier_semaphore()
    for other in others:
        pl.semaphore_signal(barrier, inc=1, device_id={"wid": other}, device_id_type=MESH)
    pl.semaphore_wait(barrier, len(others))


def send(src, dst, send_sem, recv_sem, to):
    copy = pltpu.make_async_remote_copy(
        src_ref=src,
        dst_ref=dst,
        send_sem=send_sem,
        recv_sem=recv_sem,
        device_id={"wid": to},
        device_id_type=MESH,
    )
    copy.start()
    return copy


def scatter_sums(part_ref, got_y, mine, got_z, sems, place):
    hi, y, partner, peers = place
    copies = [
        send(part_ref.at[:, (y + d) % 4], got_y.at[d - 1], sems.at[0, d - 1], sems.at[1, d - 1], peers[d - 1])
        for d in (1, 2, 3)
    ]
    for copy in copies:
        copy.wait()

    def total(h):
        s = part_ref[h, y].astype(jnp.float32)
        for d in range(3):
            s = s + got_y[d, h].astype(jnp.float32)
        return s

    mine[...] = total(1 - hi).astype(mine.dtype)
    copy = send(mine, got_z, sems.at[0, 3], sems.at[1, 3], partner)
    own = total(hi)
    copy.wait()
    return own + got_z[...].astype(jnp.float32)


def gather_start(out_ref, sems, base, place):
    hi, y, partner, peers = place
    block = out_ref.at[hi, y]
    far = send(block, block, sems.at[0, base], sems.at[1, base], partner)
    near = [
        send(block, block, sems.at[0, base + d], sems.at[1, base + d], peers[d - 1]) for d in (1, 2, 3)
    ]
    return far, near


def gather_pass(out_ref, sems, base, far, place):
    hi, y, partner, peers = place
    far.wait()
    block = out_ref.at[1 - hi, y]
    return [
        send(block, block, sems.at[0, base + 3 + d], sems.at[1, base + 3 + d], peers[d - 1])
        for d in (1, 2, 3)
    ]


def forward_kernel(part_ref, sq_ref, bias_ref, live_ref, codes_ref, pre_ref, own_ref, row_ref,
                   got_y, mine, got_z, sq_y, sq_mine, sq_z, sems):
    place = wid_place()
    hi, y, partner, peers = place
    greet([partner] + peers)
    sq_copies = [
        send(sq_ref, sq_y.at[d - 1], sems.at[0, 10 + d], sems.at[1, 10 + d], peers[d - 1]) for d in (1, 2, 3)
    ]
    for copy in sq_copies:
        copy.wait()
    sq_mine[...] = sq_ref[...] + sq_y[0] + sq_y[1] + sq_y[2]
    sq_far = send(sq_mine, sq_z, sems.at[0, 14], sems.at[1, 14], partner)
    preact = scatter_sums(part_ref, got_y, mine, got_z, sems, place) + bias_ref[...]
    pre_ref[...] = preact
    codes = (gelu(preact) * live_ref[...]).astype(jnp.bfloat16)
    own_ref[...] = codes
    codes_ref[hi, y] = codes
    far, near = gather_start(codes_ref, sems, 4, place)
    sq_far.wait()
    row_ref[...] = sq_mine[...] + sq_z[...]
    late = gather_pass(codes_ref, sems, 4, far, place)
    for copy in near + late:
        copy.wait()


def backward_kernel(part_ref, pre_ref, own_ref, live_ref, dpre_ref, small_ref, got_y, mine, got_z, sems):
    place = wid_place()
    hi, y, partner, peers = place
    greet([partner] + peers)
    dcode = scatter_sums(part_ref, got_y, mine, got_z, sems, place)
    dpre = dcode * gelu_slope(pre_ref[...]) * live_ref[...]
    dpre_ref[hi, y] = dpre.astype(jnp.bfloat16)
    far, near = gather_start(dpre_ref, sems, 4, place)
    along = jnp.sum(own_ref[...].astype(jnp.float32) * dcode, axis=0, keepdims=True)
    bias_grad = jnp.sum(dpre, axis=0, keepdims=True)
    row = lax.broadcasted_iota(jnp.int32, (8, BS), 0)
    small_ref[hi, y] = jnp.where(row == 0, along, bias_grad)
    small_far, small_near = gather_start(small_ref, sems, 11, place)
    late = gather_pass(dpre_ref, sems, 4, far, place)
    small_late = gather_pass(small_ref, sems, 11, small_far, place)
    for copy in near + late + small_near + small_late:
        copy.wait()


def vmem(n):
    return [pl.BlockSpec(memory_space=pltpu.VMEM)] * n


def sum_scratch(slots):
    return [
        pltpu.VMEM((3, 2, slots, BS), jnp.bfloat16),
        pltpu.VMEM((slots, BS), jnp.bfloat16),
        pltpu.VMEM((slots, BS), jnp.bfloat16),
    ]


def forward_sums(part, sq, bias, live):
    slots = part.shape[2]
    return pl.pallas_call(
        forward_kernel,
        out_shape=(
            jax.ShapeDtypeStruct((2, 4, slots, BS), jnp.bfloat16),
            jax.ShapeDtypeStruct((slots, BS), jnp.float32),
            jax.ShapeDtypeStruct((slots, BS), jnp.bfloat16),
            jax.ShapeDtypeStruct((8, BS), jnp.float32),
        ),
        in_specs=vmem(4),
        out_specs=tuple(vmem(4)),
        scratch_shapes=sum_scratch(slots)
        + [
            pltpu.VMEM((3, 8, BS), jnp.float32),
            pltpu.VMEM((8, BS), jnp.float32),
            pltpu.VMEM((8, BS), jnp.float32),
            pltpu.SemaphoreType.DMA((2, 15)),
        ],
        compiler_params=pltpu.CompilerParams(collective_id=0, has_side_effects=True),
        name="forward_sums",
    )(part, sq, bias, live)


def backward_sums(part, pre, own, live):
    slots = part.shape[2]
    return pl.pallas_call(
        backward_kernel,
        out_shape=(
            jax.ShapeDtypeStruct((2, 4, slots, BS), jnp.bfloat16),
            jax.ShapeDtypeStruct((2, 4, 8, BS), jnp.float32),
        ),
        in_specs=vmem(4),
        out_specs=tuple(vmem(2)),
        scratch_shapes=sum_scratch(slots) + [pltpu.SemaphoreType.DMA((2, 18))],
        compiler_params=pltpu.CompilerParams(collective_id=1, has_side_effects=True),
        name="backward_sums",
    )(part, pre, own, live)


def lat_place():
    me = lax.axis_index("lat")
    return me // PLANE, me % PLANE


def greet_lat(place):
    z, q = place
    barrier = pltpu.get_barrier_semaphore()

    def signal(other):
        pl.semaphore_signal(barrier, inc=1, device_id={"lat": other}, device_id_type=MESH)

    for e in range(1, PLANE):
        signal(z * PLANE + (q + e) % PLANE)

    @pl.when(z > 0)
    def _():
        signal((z - 1) * PLANE + q)

    @pl.when(z < LINE - 1)
    def _():
        signal((z + 1) * PLANE + q)

    inner = jnp.logical_and(z > 0, z < LINE - 1)

    @pl.when(inner)
    def _():
        pl.semaphore_wait(barrier, PLANE + 1)

    @pl.when(jnp.logical_not(inner))
    def _():
        pl.semaphore_wait(barrier, PLANE)


def lat_copy(src, dst, send_sem, recv_sem, z, q):
    return pltpu.make_async_remote_copy(
        src_ref=src,
        dst_ref=dst,
        send_sem=send_sem,
        recv_sem=recv_sem,
        device_id={"lat": z * PLANE + q},
        device_id_type=MESH,
    )


def half(c, features):
    return pl.ds(c * (features // 2), features // 2)


def slot_matrix(local):
    spots = lax.broadcasted_iota(jnp.int32, (BS, BS), 0).astype(jnp.float32)
    hit = jnp.zeros((BS, BS), jnp.float32)
    for j in range(4):
        hit = hit + jnp.where(spots == local[j : j + 1, :], 1.0, 0.0)
    return hit


def swap_matrix():
    r = lax.broadcasted_iota(jnp.int32, (BS, BS), 0)
    col = lax.broadcasted_iota(jnp.int32, (BS, BS), 1)
    source = ((r >> 1) & 7) * 16 + (r >> 4) * 2 + (r & 1)
    return jnp.where(source == col, 1.0, 0.0).astype(jnp.bfloat16)


def spread(x_ref, all_ref, pos_ref, stage, got, out_ref, line_sems, plane_sems, place, first):
    z, q = place
    rows = BS
    features = x_ref.shape[1]

    def line_copy(b, step, c, way, src=None):
        src = all_ref.at[b] if src is None else src
        return lat_copy(
            src.at[:, half(c, features)],
            all_ref.at[b, :, half(c, features)],
            line_sems.at[0, way, step, c],
            line_sems.at[1, way, step, c],
            z + 1 - 2 * way,
            q,
        )

    def plane_copy(b, e):
        to = (q + e) % PLANE
        return lat_copy(
            stage.at[b, to], got.at[q, b], plane_sems.at[0, b, e - 1], plane_sems.at[1, b, e - 1], z, to
        )

    def select(b, ref):
        if first:
            code = ref[rows : rows + 8, 0:BS].astype(jnp.float32)
            base = (z * BS).astype(jnp.float32)
            local = code[0:4] * 8.0 + code[4:8] - base
            pos_ref[b] = jnp.concatenate([local, local], axis=0)
        else:
            local = pos_ref[b]
        hit = slot_matrix(local)
        picked = jnp.dot(hit.astype(jnp.bfloat16), ref[0:rows, :], preferred_element_type=jnp.float32)
        if first:
            filled = jnp.sum(hit, axis=1, keepdims=True)
            picked = jnp.where(filled > 0.5, picked, FILLER)
        stage[b] = picked.astype(jnp.bfloat16).reshape(PLANE, 16, features)
        got[q, b] = stage[b, q]
        for e in range(1, PLANE):
            plane_copy(b, e).start()

    can_right, can_left = z < LINE - 1, z > 0
    for c in range(2):
        @pl.when(can_right)
        def _():
            line_copy(z, 0, c, 0, x_ref).start()

        @pl.when(can_left)
        def _():
            line_copy(z, 0, c, 1, x_ref).start()

    select(z, x_ref)

    def advance(step, _):
        from_left, from_right = z - step, z + step
        for c in range(2):
            @pl.when(from_left >= 0)
            def _():
                line_copy(from_left, step - 1, c, 0).wait_recv()

                @pl.when(can_right)
                def _():
                    line_copy(from_left, step, c, 0).start()

            @pl.when(from_right < LINE)
            def _():
                line_copy(from_right, step - 1, c, 1).wait_recv()

                @pl.when(can_left)
                def _():
                    line_copy(from_right, step, c, 1).start()

        @pl.when(from_left >= 0)
        def _():
            select(from_left, all_ref.at[from_left])

        @pl.when(from_right < LINE)
        def _():
            select(from_right, all_ref.at[from_right])

        return 0

    lax.fori_loop(1, LINE, advance, 0)

    def drain(step, _):
        for c in range(2):
            @pl.when(jnp.logical_and(z - step >= 0, can_right))
            def _():
                line_copy(z - step, step, c, 0).wait_send()

            @pl.when(jnp.logical_and(z + step < LINE, can_left))
            def _():
                line_copy(z + step, step, c, 1).wait_send()

        for e in range(1, PLANE):
            plane_copy(step, e).wait()
        return 0

    lax.fori_loop(0, LINE, drain, 0)
    swap = swap_matrix()
    for source in range(PLANE):
        block = jnp.dot(
            swap, got[source].reshape(BS, features), preferred_element_type=jnp.float32
        ).astype(jnp.bfloat16)
        out_ref[:, source] = block.reshape(8, 16, features)


def collect(terms_ref, act_ref, pos_ref, res_ref, stage, got, sums, from_left, from_right, right_sum,
            left_sum, line_sems, plane_sems, place):
    z, q = place
    features = act_ref.shape[1]
    swap = swap_matrix()
    for e in range(PLANE):
        to = (q + e) % PLANE
        block = jnp.dot(
            swap, terms_ref[:, to].reshape(BS, features), preferred_element_type=jnp.float32
        ).astype(jnp.bfloat16)
        if e == 0:
            got[q] = block.reshape(LINE, 16, features)
        else:
            stage[to] = block.reshape(LINE, 16, features)

    def plane_copy(d, e):
        to = (q + e) % PLANE
        return lat_copy(
            stage.at[to, d], got.at[q, d], plane_sems.at[0, d, e - 1], plane_sems.at[1, d, e - 1], z, to
        )

    def line_copy(d, far, c, way):
        land = from_right if way else from_left
        return lat_copy(
            sums.at[d, :, half(c, features)],
            land.at[d, :, half(c, features)],
            line_sems.at[0, way, far, c],
            line_sems.at[1, way, far, c],
            z + 1 - 2 * way,
            q,
        )

    def send_out(i, _):
        far = LINE - 1 - i

        @pl.when(z + far < LINE)
        def _():
            for e in range(1, PLANE):
                plane_copy(z + far, e).start()

        @pl.when(jnp.logical_and(z - far >= 0, far > 0))
        def _():
            for e in range(1, PLANE):
                plane_copy(z - far, e).start()

        return 0

    lax.fori_loop(0, LINE, send_out, 0)

    def partial(d):
        for e in range(1, PLANE):
            plane_copy(d, e).wait_recv()
        hit = slot_matrix(pos_ref[d]).astype(jnp.bfloat16)
        terms = got[:, d].reshape(BS, features)
        return lax.dot_general(
            hit, terms, (((0,), (0,)), ((), ())), preferred_element_type=jnp.float32
        )

    def advance(i, _):
        far = LINE - 1 - i
        right, left = z + far, z - far
        go_right, go_left = right < LINE, left >= 0

        @pl.when(go_right)
        def _():
            right_sum[...] = partial(right)

        @pl.when(go_left)
        def _():
            left_sum[...] = partial(left)

        for c in range(2):
            part = half(c, features)

            @pl.when(go_right)
            def _():
                @pl.when(z > 0)
                def _():
                    line_copy(right, far + 1, c, 0).wait_recv()
                    right_sum[:, part] += from_left[right, :, part].astype(jnp.float32)

                sums[right, :, part] = right_sum[:, part].astype(jnp.bfloat16)
                line_copy(right, far, c, 0).start()

            @pl.when(go_left)
            def _():
                @pl.when(z < LINE - 1)
                def _():
                    line_copy(left, far + 1, c, 1).wait_recv()
                    left_sum[:, part] += from_right[left, :, part].astype(jnp.float32)

                sums[left, :, part] = left_sum[:, part].astype(jnp.bfloat16)
                line_copy(left, far, c, 1).start()

        return 0

    lax.fori_loop(0, LINE - 1, advance, 0)
    right_sum[...] = partial(z) - act_ref[...].astype(jnp.float32)

    @pl.when(z > 0)
    def _():
        for c in range(2):
            line_copy(z, 1, c, 0).wait_recv()
        right_sum[...] += from_left[z].astype(jnp.float32)

    @pl.when(z < LINE - 1)
    def _():
        for c in range(2):
            line_copy(z, 1, c, 1).wait_recv()
        right_sum[...] += from_right[z].astype(jnp.float32)

    res_ref[...] = right_sum[...].astype(jnp.bfloat16)

    def drain(far, _):
        for c in range(2):
            @pl.when(jnp.logical_and(z + far < LINE, far > 0))
            def _():
                line_copy(z + far, far, c, 0).wait_send()

            @pl.when(jnp.logical_and(z - far >= 0, far > 0))
            def _():
                line_copy(z - far, far, c, 1).wait_send()

        for e in range(1, PLANE):
            plane_copy(far, e).wait_send()
        return 0

    return drain


def spread_kernel(x_ref, out_ref, pos_ref, all_ref, stage, got, line_sems, plane_sems):
    place = lat_place()
    greet_lat(place)
    spread(x_ref, all_ref, pos_ref, stage, got, out_ref, line_sems, plane_sems, place, True)


def residual_kernel(terms_ref, act_ref, pos_ref, out_ref, res_ref, stage_t, got_t, sums, from_left,
                    from_right, right_sum, left_sum, all_ref, stage, got, line_t, plane_t, line_sems,
                    plane_sems):
    place = lat_place()
    greet_lat(place)
    drain = collect(terms_ref, act_ref, pos_ref, res_ref, stage_t, got_t, sums, from_left, from_right,
                    right_sum, left_sum, line_t, plane_t, place)
    spread(res_ref, all_ref, pos_ref, stage, got, out_ref, line_sems, plane_sems, place, False)
    lax.fori_loop(0, LINE, drain, 0)


def slots_buffer(features):
    return pltpu.VMEM((8, 8, 16, features), jnp.bfloat16)


def lat_sems():
    return [pltpu.SemaphoreType.DMA((2, 2, LINE, 2)), pltpu.SemaphoreType.DMA((2, LINE, PLANE - 1))]


def spread_rows(x):
    rows, features = x.shape
    return pl.pallas_call(
        spread_kernel,
        out_shape=(
            jax.ShapeDtypeStruct((8, PLANE, 16, features), jnp.bfloat16),
            jax.ShapeDtypeStruct((LINE, 8, BS), jnp.float32),
        ),
        in_specs=vmem(1),
        out_specs=tuple(vmem(2)),
        scratch_shapes=[
            pltpu.VMEM((LINE, rows, features), jnp.bfloat16),
            slots_buffer(features),
            slots_buffer(features),
        ]
        + lat_sems(),
        compiler_params=pltpu.CompilerParams(collective_id=2, has_side_effects=True),
        name="spread_rows",
    )(x)


def spread_residual(terms, activations, pos):
    rows, features = activations.shape
    row_blocks = pltpu.VMEM((LINE, rows, features), jnp.bfloat16)
    return pl.pallas_call(
        residual_kernel,
        out_shape=jax.ShapeDtypeStruct((8, PLANE, 16, features), jnp.bfloat16),
        in_specs=vmem(3),
        out_specs=vmem(1)[0],
        scratch_shapes=[
            pltpu.VMEM((rows, features), jnp.bfloat16),
            slots_buffer(features),
            slots_buffer(features),
            row_blocks,
            row_blocks,
            row_blocks,
            pltpu.VMEM((rows, features), jnp.float32),
            pltpu.VMEM((rows, features), jnp.float32),
            row_blocks,
            slots_buffer(features),
            slots_buffer(features),
        ]
        + lat_sems()
        + lat_sems(),
        compiler_params=pltpu.CompilerParams(collective_id=3, has_side_effects=True),
        name="spread_residual",
    )(terms, activations, pos)


def body(activations, block_ids, alive_tallies, encoder, encoder_bias, decoder):
    rows, features = activations.shape
    slots = block_ids.shape[1]
    lat = lax.axis_size("lat")
    wid = lax.axis_index("wid")
    f32 = jnp.float32

    flat = block_ids.reshape(rows * slots)
    order = jnp.arange(rows * slots, dtype=jnp.int32)
    earlier = (flat[:, None] == flat[None, :]) & (order[None, :] < order[:, None])
    rank = jnp.sum(earlier.astype(jnp.int32), axis=1).reshape(rows, slots)
    alive = jnp.arange(slots, dtype=jnp.int32)[None, :] < alive_tallies[:, None]
    position = block_ids * 2 + rank
    high = jnp.where(alive, position >> 3, 255)
    codes_of_rows = jnp.concatenate([high, position & 7], axis=1).T.astype(jnp.bfloat16)
    extra = jnp.pad(codes_of_rows, ((0, 8), (0, features - rows)))
    incoming, pos = spread_rows(jnp.concatenate([activations, extra], axis=0))
    incoming = incoming.reshape(8, lat * 2, features)
    live = (incoming[:, :, 0] < 1.5).astype(f32)
    own_live = jnp.broadcast_to(
        lax.dynamic_index_in_dim(live, wid, 0, keepdims=False)[:, None], (lat * 2, BS)
    )

    decoder_wide = decoder.astype(f32)
    local_sq = jnp.sum(jnp.square(decoder_wide), axis=1).reshape(8, BS)
    encoder_blocks = encoder.reshape(features, 8, BS)
    partial_pre = jnp.einsum(
        "aec,caw->aew", incoming, encoder_blocks, preferred_element_type=f32
    ).astype(jnp.bfloat16)
    own_bias = lax.dynamic_index_in_dim(encoder_bias.reshape(8, BS), wid, 0, keepdims=True)
    codes, own_pre, own_codes, row_sq = forward_sums(
        partial_pre.reshape(2, 4, lat * 2, BS), local_sq, own_bias, own_live
    )
    codes = codes.reshape(8, lat * 2, BS)
    row_norm = jnp.sqrt(row_sq + EPS)[:, :, None]
    unit = (decoder_wide.reshape(8, BS, features) / row_norm).astype(jnp.bfloat16)

    terms = jnp.einsum("jkr,jrs->jks", codes, unit, preferred_element_type=f32).astype(jnp.bfloat16)
    resid_in = spread_residual(terms.reshape(8, PLANE, 16, features), activations, pos)
    resid_in = resid_in.reshape(8, lat * 2, features)

    partial_dcode = jnp.einsum(
        "zea,zxa->zex", resid_in, unit, preferred_element_type=f32
    ).astype(jnp.bfloat16)
    dpre, small = backward_sums(
        partial_dcode.reshape(2, 4, lat * 2, BS), own_pre, own_codes, own_live
    )
    dpre = dpre.reshape(8, lat * 2, BS)
    small = small.reshape(8, 8, BS)
    raw = jnp.einsum("ekc,ekv->ecv", codes, resid_in, preferred_element_type=f32)
    along = small[:, 0, :, None]
    bias_grad = small[:, 1].reshape(8 * BS)
    encoder_grad = (
        jnp.einsum("kiy,kif->ykf", incoming, dpre, preferred_element_type=f32)
        .reshape(features, 8 * BS)
        .astype(jnp.bfloat16)
    )
    decoder_grad = (
        ((raw - along * unit.astype(f32)) / row_norm).astype(jnp.bfloat16).reshape(8 * BS, features)
    )
    return encoder_grad, decoder_grad, bias_grad


def solution(mesh):
    return jax.shard_map(
        body,
        mesh=mesh,
        in_specs=(
            P("lat", "wid"),
            P("lat", None),
            P("lat"),
            P("wid", "lat"),
            P("lat"),
            P("lat", "wid"),
        ),
        out_specs=(P("wid", "lat"), P("lat", "wid"), P("lat")),
        check_vma=False,
    )
```

```python
import jax
import jax.numpy as jnp
from jax import lax
from jax.experimental import pallas as pl
from jax.experimental.pallas import tpu as pltpu
from jax.sharding import PartitionSpec as P

BS = 128
EPS = 1e-06
C0 = 0.7978845608
C1 = 0.044715
FILLER = 2.0
LINE = 8
PLANE = 8
MESH = pl.DeviceIdType.MESH


def gelu(v):
    return 0.5 * v * (1.0 + jnp.tanh(C0 * (v + C1 * v * v * v)))


def gelu_slope(v):
    t = jnp.tanh(C0 * (v + C1 * v * v * v))
    return 0.5 * (1.0 + t) + 0.5 * v * (1.0 - t * t) * C0 * (1.0 + 3.0 * C1 * v * v)


def wid_place():
    me = lax.axis_index("wid")
    hi, y = me // 4, me % 4
    partner = (1 - hi) * 4 + y
    peers = [hi * 4 + (y + d) % 4 for d in (1, 2, 3)]
    return hi, y, partner, peers


def send(src, dst, send_sem, recv_sem, to):
    copy = pltpu.make_async_remote_copy(
        src_ref=src,
        dst_ref=dst,
        send_sem=send_sem,
        recv_sem=recv_sem,
        device_id={"wid": to},
        device_id_type=MESH,
    )
    copy.start()
    return copy


def scatter_sums(part_ref, got_y, mine, got_z, sems, place, meanwhile=None):
    hi, y, partner, peers = place
    copies = [
        send(part_ref.at[:, (y + d) % 4], got_y.at[d - 1], sems.at[0, d - 1], sems.at[1, d - 1], peers[d - 1])
        for d in (1, 2, 3)
    ]
    if meanwhile is not None:
        meanwhile()
    for copy in copies:
        copy.wait()

    def total(h):
        s = part_ref[h, y].astype(jnp.float32)
        for d in range(3):
            s = s + got_y[d, h].astype(jnp.float32)
        return s

    mine[...] = total(1 - hi).astype(mine.dtype)
    copy = send(mine, got_z, sems.at[0, 3], sems.at[1, 3], partner)
    own = total(hi)
    copy.wait()
    return own + got_z[...].astype(jnp.float32)


def gather_start(out_ref, sems, base, place):
    hi, y, partner, peers = place
    block = out_ref.at[hi, y]
    far = send(block, block, sems.at[0, base], sems.at[1, base], partner)
    near = [
        send(block, block, sems.at[0, base + d], sems.at[1, base + d], peers[d - 1]) for d in (1, 2, 3)
    ]
    return far, near


def gather_pass(out_ref, sems, base, far, place):
    hi, y, partner, peers = place
    far.wait()
    block = out_ref.at[1 - hi, y]
    return [
        send(block, block, sems.at[0, base + 3 + d], sems.at[1, base + 3 + d], peers[d - 1])
        for d in (1, 2, 3)
    ]


def vmem(n):
    return [pl.BlockSpec(memory_space=pltpu.VMEM)] * n


def sum_scratch(slots):
    return [
        pltpu.VMEM((3, 2, slots, BS), jnp.bfloat16),
        pltpu.VMEM((slots, BS), jnp.bfloat16),
        pltpu.VMEM((slots, BS), jnp.bfloat16),
    ]


def lat_place():
    me = lax.axis_index("lat")
    return me // PLANE, me % PLANE


def greet(place, wid):
    z, q = place
    _, _, partner, peers = wid
    barrier = pltpu.get_barrier_semaphore()

    def signal(**other):
        pl.semaphore_signal(barrier, inc=1, device_id=other, device_id_type=MESH)

    for other in [partner] + peers:
        signal(wid=other)
    for e in range(1, PLANE):
        signal(lat=z * PLANE + (q + e) % PLANE)

    @pl.when(z > 0)
    def _():
        signal(lat=(z - 1) * PLANE + q)

    @pl.when(z < LINE - 1)
    def _():
        signal(lat=(z + 1) * PLANE + q)

    inner = jnp.logical_and(z > 0, z < LINE - 1)

    @pl.when(inner)
    def _():
        pl.semaphore_wait(barrier, PLANE + 5)

    @pl.when(jnp.logical_not(inner))
    def _():
        pl.semaphore_wait(barrier, PLANE + 4)


def lat_copy(src, dst, send_sem, recv_sem, z, q):
    return pltpu.make_async_remote_copy(
        src_ref=src,
        dst_ref=dst,
        send_sem=send_sem,
        recv_sem=recv_sem,
        device_id={"lat": z * PLANE + q},
        device_id_type=MESH,
    )


def half(c, features):
    return pl.ds(c * (features // 2), features // 2)


def slot_matrix(local):
    spots = lax.broadcasted_iota(jnp.int32, (BS, BS), 0).astype(jnp.float32)
    hit = jnp.zeros((BS, BS), jnp.float32)
    for j in range(4):
        hit = hit + jnp.where(spots == local[j : j + 1, :], 1.0, 0.0)
    return hit


def swap_matrix():
    r = lax.broadcasted_iota(jnp.int32, (BS, BS), 0)
    col = lax.broadcasted_iota(jnp.int32, (BS, BS), 1)
    source = ((r >> 1) & 7) * 16 + (r >> 4) * 2 + (r & 1)
    return jnp.where(source == col, 1.0, 0.0).astype(jnp.bfloat16)


def spread(x_ref, all_ref, pos_ref, stage, got, out_ref, line_sems, plane_sems, place, first, meanwhile=None):
    z, q = place
    rows = BS
    features = x_ref.shape[1]

    def line_copy(b, step, c, way, src=None):
        src = all_ref.at[b] if src is None else src
        height = pl.ds(0, rows if c else x_ref.shape[0])
        return lat_copy(
            src.at[height, half(c, features)],
            all_ref.at[b, height, half(c, features)],
            line_sems.at[0, way, step, c],
            line_sems.at[1, way, step, c],
            z + 1 - 2 * way,
            q,
        )

    def plane_copy(b, e):
        to = (q + e) % PLANE
        return lat_copy(
            stage.at[b, to], got.at[q, b], plane_sems.at[0, b, e - 1], plane_sems.at[1, b, e - 1], z, to
        )

    def select(b, ref):
        if first:
            code = ref[rows : rows + 8, 0:BS].astype(jnp.float32)
            base = (z * BS).astype(jnp.float32)
            local = code[0:4] * 8.0 + code[4:8] - base
            pos_ref[b] = jnp.concatenate([local, local], axis=0)
        else:
            local = pos_ref[b]
        hit = slot_matrix(local)
        picked = jnp.dot(hit.astype(jnp.bfloat16), ref[0:rows, :], preferred_element_type=jnp.float32)
        if first:
            filled = jnp.sum(hit, axis=1, keepdims=True)
            picked = jnp.where(filled > 0.5, picked, FILLER)
        stage[b] = picked.astype(jnp.bfloat16).reshape(PLANE, 16, features)
        got[q, b] = stage[b, q]
        for e in range(1, PLANE):
            plane_copy(b, e).start()

    can_right, can_left = z < LINE - 1, z > 0
    for c in range(2):
        @pl.when(can_right)
        def _():
            line_copy(z, 0, c, 0, x_ref).start()

        @pl.when(can_left)
        def _():
            line_copy(z, 0, c, 1, x_ref).start()

    select(z, x_ref)
    if meanwhile is not None:
        meanwhile()

    def advance(step, _):
        from_left, from_right = z - step, z + step
        for c in range(2):
            @pl.when(from_left >= 0)
            def _():
                line_copy(from_left, step - 1, c, 0).wait_recv()

                @pl.when(can_right)
                def _():
                    line_copy(from_left, step, c, 0).start()

            @pl.when(from_right < LINE)
            def _():
                line_copy(from_right, step - 1, c, 1).wait_recv()

                @pl.when(can_left)
                def _():
                    line_copy(from_right, step, c, 1).start()

        @pl.when(from_left >= 0)
        def _():
            select(from_left, all_ref.at[from_left])

        @pl.when(from_right < LINE)
        def _():
            select(from_right, all_ref.at[from_right])

        return 0

    lax.fori_loop(1, LINE, advance, 0)

    def drain(step, _):
        for c in range(2):
            @pl.when(jnp.logical_and(z - step >= 0, can_right))
            def _():
                line_copy(z - step, step, c, 0).wait_send()

            @pl.when(jnp.logical_and(z + step < LINE, can_left))
            def _():
                line_copy(z + step, step, c, 1).wait_send()

        for e in range(1, PLANE):
            plane_copy(step, e).wait()
        return 0

    lax.fori_loop(0, LINE, drain, 0)
    swap = swap_matrix()
    for source in range(PLANE):
        block = jnp.dot(
            swap, got[source].reshape(BS, features), preferred_element_type=jnp.float32
        ).astype(jnp.bfloat16)
        out_ref[:, source] = block.reshape(8, 16, features)


def collect(terms_ref, act_ref, pos_ref, res_ref, stage, got, sums, from_left, from_right, right_sum,
            left_sum, line_sems, plane_sems, place):
    z, q = place
    features = act_ref.shape[1]
    swap = swap_matrix()
    for e in range(PLANE):
        to = (q + e) % PLANE
        block = jnp.dot(
            swap, terms_ref[:, to].reshape(BS, features), preferred_element_type=jnp.float32
        ).astype(jnp.bfloat16)
        if e == 0:
            got[q] = block.reshape(LINE, 16, features)
        else:
            stage[to] = block.reshape(LINE, 16, features)

    def plane_copy(d, e):
        to = (q + e) % PLANE
        return lat_copy(
            stage.at[to, d], got.at[q, d], plane_sems.at[0, d, e - 1], plane_sems.at[1, d, e - 1], z, to
        )

    def line_copy(d, far, c, way):
        land = from_right if way else from_left
        return lat_copy(
            sums.at[d, :, half(c, features)],
            land.at[d, :, half(c, features)],
            line_sems.at[0, way, far, c],
            line_sems.at[1, way, far, c],
            z + 1 - 2 * way,
            q,
        )

    def send_out(i, _):
        far = LINE - 1 - i

        @pl.when(z + far < LINE)
        def _():
            for e in range(1, PLANE):
                plane_copy(z + far, e).start()

        @pl.when(jnp.logical_and(z - far >= 0, far > 0))
        def _():
            for e in range(1, PLANE):
                plane_copy(z - far, e).start()

        return 0

    lax.fori_loop(0, LINE, send_out, 0)

    def partial(d):
        for e in range(1, PLANE):
            plane_copy(d, e).wait_recv()
        hit = slot_matrix(pos_ref[d]).astype(jnp.bfloat16)
        terms = got[:, d].reshape(BS, features)
        return lax.dot_general(
            hit, terms, (((0,), (0,)), ((), ())), preferred_element_type=jnp.float32
        )

    def advance(i, _):
        far = LINE - 1 - i
        right, left = z + far, z - far
        go_right, go_left = right < LINE, left >= 0

        @pl.when(go_right)
        def _():
            right_sum[...] = partial(right)

        @pl.when(go_left)
        def _():
            left_sum[...] = partial(left)

        for c in range(2):
            part = half(c, features)

            @pl.when(go_right)
            def _():
                @pl.when(z > 0)
                def _():
                    line_copy(right, far + 1, c, 0).wait_recv()
                    right_sum[:, part] += from_left[right, :, part].astype(jnp.float32)

                sums[right, :, part] = right_sum[:, part].astype(jnp.bfloat16)
                line_copy(right, far, c, 0).start()

            @pl.when(go_left)
            def _():
                @pl.when(z < LINE - 1)
                def _():
                    line_copy(left, far + 1, c, 1).wait_recv()
                    left_sum[:, part] += from_right[left, :, part].astype(jnp.float32)

                sums[left, :, part] = left_sum[:, part].astype(jnp.bfloat16)
                line_copy(left, far, c, 1).start()

        return 0

    lax.fori_loop(0, LINE - 1, advance, 0)
    right_sum[...] = partial(z) - act_ref[...].astype(jnp.float32)

    @pl.when(z > 0)
    def _():
        for c in range(2):
            line_copy(z, 1, c, 0).wait_recv()
        right_sum[...] += from_left[z].astype(jnp.float32)

    @pl.when(z < LINE - 1)
    def _():
        for c in range(2):
            line_copy(z, 1, c, 1).wait_recv()
        right_sum[...] += from_right[z].astype(jnp.float32)

    res_ref[...] = right_sum[...].astype(jnp.bfloat16)

    def drain(far, _):
        for c in range(2):
            @pl.when(jnp.logical_and(z + far < LINE, far > 0))
            def _():
                line_copy(z + far, far, c, 0).wait_send()

            @pl.when(jnp.logical_and(z - far >= 0, far > 0))
            def _():
                line_copy(z - far, far, c, 1).wait_send()

        for e in range(1, PLANE):
            plane_copy(far, e).wait_send()
        return 0

    return drain


def column(row):
    r = lax.broadcasted_iota(jnp.int32, (BS, BS), 0)
    col = lax.broadcasted_iota(jnp.int32, (BS, BS), 1)
    return jnp.sum(jnp.where(r == col, row, 0.0), axis=1, keepdims=True)


def step_kernel(x_ref, sq_ref, bias_ref, enc_ref, dec_ref,
                in_ref, resid_ref, codes_ref, dpre_ref, unit_ref, row_ref, small_ref,
                all_a, stage_a, got_a, line_a, plane_a,
                sq_y, sq_mine, sq_z,
                part_b, got_yb, mine_b, got_zb, pre_ref, own_ref, sems_b,
                terms_ref, res_ref, stage_c, got_c, sums, from_left, from_right, right_sum, left_sum,
                line_c, plane_c,
                all_d, stage_d, got_d, line_d, plane_d,
                part_e, got_ye, mine_e, got_ze, sems_e, pos_ref):
    place = lat_place()
    wid = wid_place()
    hi, y, partner, peers = wid
    rows = BS
    features = x_ref.shape[1]
    f32, bf16 = jnp.float32, jnp.bfloat16
    greet(place, wid)

    sq_copies = [
        send(sq_ref, sq_y.at[d - 1], sems_b.at[0, 10 + d], sems_b.at[1, 10 + d], peers[d - 1])
        for d in (1, 2, 3)
    ]
    sq_far = pltpu.make_async_remote_copy(
        src_ref=sq_mine, dst_ref=sq_z, send_sem=sems_b.at[0, 14], recv_sem=sems_b.at[1, 14],
        device_id={"wid": partner}, device_id_type=MESH,
    )

    def sum_squares():
        for copy in sq_copies:
            copy.wait()
        sq_mine[...] = sq_ref[...] + sq_y[0] + sq_y[1] + sq_y[2]
        sq_far.start()

    spread(x_ref, all_a, pos_ref, stage_a, got_a, in_ref, line_a, plane_a, place, True, sum_squares)

    for k in range(8):
        part_b[k // 4, k % 4] = jnp.dot(
            in_ref[k].reshape(BS, features), enc_ref[:, k * BS : (k + 1) * BS], preferred_element_type=f32
        ).astype(bf16)

    def normalize():
        sq_far.wait()
        row_ref[...] = jnp.sqrt(sq_mine[...] + sq_z[...] + EPS)
        for k in range(8):
            norm = column(row_ref[k : k + 1, :])
            unit_ref[k] = (dec_ref[k].astype(f32) / norm).astype(bf16)

    mine = hi * 4 + y
    preact = scatter_sums(part_b, got_yb, mine_b, got_zb, sems_b, wid, normalize) + bias_ref[mine]
    pre_ref[...] = preact
    live = in_ref[mine].reshape(BS, features)[:, 0:1].astype(f32) < 1.5
    codes = jnp.where(live, gelu(preact), 0.0).astype(bf16)
    own_ref[...] = codes
    codes_ref[hi, y] = codes
    far, near = gather_start(codes_ref, sems_b, 4, wid)
    late = gather_pass(codes_ref, sems_b, 4, far, wid)
    for copy in near + late:
        copy.wait()

    for k in range(8):
        terms_ref[k] = (
            jnp.dot(codes_ref[k // 4, k % 4], unit_ref[k], preferred_element_type=f32)
            .astype(bf16)
            .reshape(PLANE, 16, features)
        )
    drain = collect(terms_ref, x_ref.at[0:rows, :], pos_ref, res_ref, stage_c, got_c, sums, from_left,
                    from_right, right_sum, left_sum, line_c, plane_c, place)
    spread(res_ref, all_d, pos_ref, stage_d, got_d, resid_ref, line_d, plane_d, place, False)

    for k in range(8):
        part_e[k // 4, k % 4] = lax.dot_general(
            resid_ref[k].reshape(BS, features), unit_ref[k], (((1,), (1,)), ((), ())),
            preferred_element_type=f32,
        ).astype(bf16)
    dcode = scatter_sums(part_e, got_ye, mine_e, got_ze, sems_e, wid)
    dpre = jnp.where(live, dcode * gelu_slope(pre_ref[...]), 0.0)
    dpre_ref[hi, y] = dpre.astype(bf16)
    far, near = gather_start(dpre_ref, sems_e, 4, wid)
    along = jnp.sum(own_ref[...].astype(f32) * dcode, axis=0, keepdims=True)
    bias_grad = jnp.sum(dpre, axis=0, keepdims=True)
    row = lax.broadcasted_iota(jnp.int32, (8, BS), 0)
    small_ref[hi, y] = jnp.where(row == 0, along, bias_grad)
    small_far, small_near = gather_start(small_ref, sems_e, 11, wid)
    lax.fori_loop(0, LINE, drain, 0)
    late = gather_pass(dpre_ref, sems_e, 4, far, wid)
    small_late = gather_pass(small_ref, sems_e, 11, small_far, wid)
    for copy in near + late + small_near + small_late:
        copy.wait()


def slots_buffer(features):
    return pltpu.VMEM((8, 8, 16, features), jnp.bfloat16)


def lat_sems():
    return [pltpu.SemaphoreType.DMA((2, 2, LINE, 2)), pltpu.SemaphoreType.DMA((2, LINE, PLANE - 1))]


def run_step(x, sq, bias, encoder, decoder):
    rows, features = BS, x.shape[1]
    f32, bf16 = jnp.float32, jnp.bfloat16
    slots = 2 * LINE * PLANE
    row_blocks = pltpu.VMEM((LINE, rows, features), bf16)
    slot = slots_buffer(features)
    wid_part = pltpu.VMEM((2, 4, slots, BS), bf16)
    sq_block = pltpu.VMEM((8, BS), f32)
    row_total = pltpu.VMEM((rows, features), f32)
    return pl.pallas_call(
        step_kernel,
        out_shape=(
            jax.ShapeDtypeStruct((8, PLANE, 16, features), bf16),
            jax.ShapeDtypeStruct((8, PLANE, 16, features), bf16),
            jax.ShapeDtypeStruct((2, 4, slots, BS), bf16),
            jax.ShapeDtypeStruct((2, 4, slots, BS), bf16),
            jax.ShapeDtypeStruct((8, BS, features), bf16),
            jax.ShapeDtypeStruct((8, BS), f32),
            jax.ShapeDtypeStruct((2, 4, 8, BS), f32),
        ),
        in_specs=vmem(5),
        out_specs=tuple(vmem(7)),
        scratch_shapes=[pltpu.VMEM((LINE, x.shape[0], features), bf16), slot, slot]
        + lat_sems()
        + [pltpu.VMEM((3, 8, BS), f32), sq_block, sq_block]
        + [wid_part]
        + sum_scratch(slots)
        + [pltpu.VMEM((slots, BS), f32), pltpu.VMEM((slots, BS), bf16), pltpu.SemaphoreType.DMA((2, 15))]
        + [slot, pltpu.VMEM((rows, features), bf16), slot, slot]
        + [row_blocks, row_blocks, row_blocks, row_total, row_total]
        + lat_sems()
        + [row_blocks, slot, slot]
        + lat_sems()
        + [wid_part]
        + sum_scratch(slots)
        + [pltpu.SemaphoreType.DMA((2, 18)), pltpu.VMEM((LINE, 8, BS), f32)],
        compiler_params=pltpu.CompilerParams(collective_id=0, has_side_effects=True),
        name="step",
    )(x, sq, bias, encoder, decoder)


def body(activations, block_ids, alive_tallies, encoder, encoder_bias, decoder):
    rows, features = activations.shape
    slots = block_ids.shape[1]
    lat = lax.axis_size("lat")
    f32 = jnp.float32

    flat = block_ids.reshape(rows * slots)
    order = jnp.arange(rows * slots, dtype=jnp.int32)
    earlier = (flat[:, None] == flat[None, :]) & (order[None, :] < order[:, None])
    rank = jnp.sum(earlier.astype(jnp.int32), axis=1).reshape(rows, slots)
    alive = jnp.arange(slots, dtype=jnp.int32)[None, :] < alive_tallies[:, None]
    position = block_ids * 2 + rank
    high = jnp.where(alive, position >> 3, 255)
    codes_of_rows = jnp.concatenate([high, position & 7], axis=1).T.astype(jnp.bfloat16)
    extra = jnp.pad(codes_of_rows, ((0, 8), (0, features - rows)))
    local_sq = jnp.sum(jnp.square(decoder.astype(f32)), axis=1).reshape(8, BS)
    incoming, resid_in, codes, dpre, unit, row_norm, small = run_step(
        jnp.concatenate([activations, extra], axis=0),
        local_sq,
        encoder_bias.reshape(8, 1, BS),
        encoder,
        decoder.reshape(8, BS, features),
    )
    incoming = incoming.reshape(8, lat * 2, features)
    resid_in = resid_in.reshape(8, lat * 2, features)
    codes = codes.reshape(8, lat * 2, BS)
    dpre = dpre.reshape(8, lat * 2, BS)
    small = small.reshape(8, 8, BS)
    row_norm = row_norm[:, :, None]
    raw = jnp.einsum("ekc,ekv->ecv", codes, resid_in, preferred_element_type=f32)
    along = small[:, 0, :, None]
    bias_grad = small[:, 1].reshape(8 * BS)
    encoder_grad = (
        jnp.einsum("kiy,kif->ykf", incoming, dpre, preferred_element_type=f32)
        .reshape(features, 8 * BS)
        .astype(jnp.bfloat16)
    )
    decoder_grad = (
        ((raw - along * unit.astype(f32)) / row_norm).astype(jnp.bfloat16).reshape(8 * BS, features)
    )
    return encoder_grad, decoder_grad, bias_grad


def solution(mesh):
    return jax.shard_map(
        body,
        mesh=mesh,
        in_specs=(
            P("lat", "wid"),
            P("lat", None),
            P("lat"),
            P("wid", "lat"),
            P("lat"),
            P("lat", "wid"),
        ),
        out_specs=(P("wid", "lat"), P("lat", "wid"), P("lat")),
        check_vma=False,
    )
```

```python
import jax
import jax.numpy as jnp
from jax import lax
from jax.experimental import pallas as pl
from jax.experimental.pallas import tpu as pltpu
from jax.sharding import PartitionSpec as P

BS = 128
EPS = 1e-06
C0 = 0.7978845608
C1 = 0.044715
FILLER = 2.0
LINE = 8
PLANE = 8
MESH = pl.DeviceIdType.MESH


def gelu(v):
    return 0.5 * v * (1.0 + jnp.tanh(C0 * (v + C1 * v * v * v)))


def gelu_slope(v):
    t = jnp.tanh(C0 * (v + C1 * v * v * v))
    return 0.5 * (1.0 + t) + 0.5 * v * (1.0 - t * t) * C0 * (1.0 + 3.0 * C1 * v * v)


def wid_place():
    me = lax.axis_index("wid")
    hi, y = me // 4, me % 4
    partner = (1 - hi) * 4 + y
    peers = [hi * 4 + (y + d) % 4 for d in (1, 2, 3)]
    return hi, y, partner, peers


def send(src, dst, send_sem, recv_sem, to):
    copy = pltpu.make_async_remote_copy(
        src_ref=src,
        dst_ref=dst,
        send_sem=send_sem,
        recv_sem=recv_sem,
        device_id={"wid": to},
        device_id_type=MESH,
    )
    copy.start()
    return copy


def wid_sum(part_ref, got_y, mine, got_z, sems, place, meanwhile, finish):
    hi, y, partner, peers = place
    near = [
        [
            send(part_ref.at[h, (y + d) % 4], got_y.at[d - 1, h], sems.at[0, 3 * h + d - 1],
                 sems.at[1, 3 * h + d - 1], peers[d - 1])
            for d in (1, 2, 3)
        ]
        for h in range(2)
    ]
    far = []
    for h in range(2):
        for copy in near[h]:
            copy.wait()
        s = part_ref[h, y].astype(jnp.float32)
        for d in range(3):
            s = s + got_y[d, h].astype(jnp.float32)
        mine[h] = s.astype(mine.dtype)
        far.append(send(mine.at[h], got_z.at[h], sems.at[0, 6 + h], sems.at[1, 6 + h], partner))
    meanwhile()
    late = []
    for h in range(2):
        far[h].wait()
        late += finish(h, mine[h].astype(jnp.float32) + got_z[h].astype(jnp.float32))
    for copy in late:
        copy.wait()


def hand_on(block, sems, base, place):
    peers = place[3]
    return [
        send(block, block, sems.at[0, base + d], sems.at[1, base + d], peers[d - 1]) for d in (1, 2, 3)
    ]


def vmem(n):
    return [pl.BlockSpec(memory_space=pltpu.VMEM)] * n


def sum_scratch(slots):
    return [
        pltpu.VMEM((3, 2, slots, BS), jnp.bfloat16),
        pltpu.VMEM((2, slots, BS), jnp.bfloat16),
        pltpu.VMEM((2, slots, BS), jnp.bfloat16),
    ]


def lat_place():
    me = lax.axis_index("lat")
    return me // PLANE, me % PLANE


def greet(place, wid):
    z, q = place
    _, _, partner, peers = wid
    barrier = pltpu.get_barrier_semaphore()

    def signal(**other):
        pl.semaphore_signal(barrier, inc=1, device_id=other, device_id_type=MESH)

    for other in [partner] + peers:
        signal(wid=other)
    for e in range(1, PLANE):
        signal(lat=z * PLANE + (q + e) % PLANE)

    @pl.when(z > 0)
    def _():
        signal(lat=(z - 1) * PLANE + q)

    @pl.when(z < LINE - 1)
    def _():
        signal(lat=(z + 1) * PLANE + q)

    inner = jnp.logical_and(z > 0, z < LINE - 1)

    @pl.when(inner)
    def _():
        pl.semaphore_wait(barrier, PLANE + 5)

    @pl.when(jnp.logical_not(inner))
    def _():
        pl.semaphore_wait(barrier, PLANE + 4)


def lat_copy(src, dst, send_sem, recv_sem, z, q):
    return pltpu.make_async_remote_copy(
        src_ref=src,
        dst_ref=dst,
        send_sem=send_sem,
        recv_sem=recv_sem,
        device_id={"lat": z * PLANE + q},
        device_id_type=MESH,
    )


def half(c, features):
    return pl.ds(c * (features // 2), features // 2)


def slot_matrix(local):
    spots = lax.broadcasted_iota(jnp.int32, (BS, BS), 0).astype(jnp.float32)
    hit = jnp.zeros((BS, BS), jnp.float32)
    for j in range(4):
        hit = hit + jnp.where(spots == local[j : j + 1, :], 1.0, 0.0)
    return hit


def swap_matrix():
    r = lax.broadcasted_iota(jnp.int32, (BS, BS), 0)
    col = lax.broadcasted_iota(jnp.int32, (BS, BS), 1)
    source = ((r >> 1) & 7) * 16 + (r >> 4) * 2 + (r & 1)
    return jnp.where(source == col, 1.0, 0.0).astype(jnp.bfloat16)


def spread(x_ref, all_ref, pos_ref, stage, got, out_ref, line_sems, plane_sems, place, first, meanwhile=None, after=None):
    z, q = place
    rows = BS
    features = x_ref.shape[1]

    def line_copy(b, step, c, way, src=None):
        src = all_ref.at[b] if src is None else src
        height = pl.ds(0, rows if c else x_ref.shape[0])
        return lat_copy(
            src.at[height, half(c, features)],
            all_ref.at[b, height, half(c, features)],
            line_sems.at[0, way, step, c],
            line_sems.at[1, way, step, c],
            z + 1 - 2 * way,
            q,
        )

    def plane_copy(b, e):
        to = (q + e) % PLANE
        return lat_copy(
            stage.at[b, to], got.at[q, b], plane_sems.at[0, b, e - 1], plane_sems.at[1, b, e - 1], z, to
        )

    def select(b, ref):
        if first:
            code = ref[rows : rows + 8, 0:BS].astype(jnp.float32)
            base = (z * BS).astype(jnp.float32)
            local = code[0:4] * 8.0 + code[4:8] - base
            pos_ref[b] = jnp.concatenate([local, local], axis=0)
        else:
            local = pos_ref[b]
        hit = slot_matrix(local)
        picked = jnp.dot(hit.astype(jnp.bfloat16), ref[0:rows, :], preferred_element_type=jnp.float32)
        if first:
            filled = jnp.sum(hit, axis=1, keepdims=True)
            picked = jnp.where(filled > 0.5, picked, FILLER)
        stage[b] = picked.astype(jnp.bfloat16).reshape(PLANE, 16, features)
        got[q, b] = stage[b, q]
        for e in range(1, PLANE):
            plane_copy(b, e).start()

    can_right, can_left = z < LINE - 1, z > 0
    for c in range(2):
        @pl.when(can_right)
        def _():
            line_copy(z, 0, c, 0, x_ref).start()

        @pl.when(can_left)
        def _():
            line_copy(z, 0, c, 1, x_ref).start()

    select(z, x_ref)
    if meanwhile is not None:
        meanwhile()

    def advance(step, _):
        from_left, from_right = z - step, z + step
        for c in range(2):
            @pl.when(from_left >= 0)
            def _():
                line_copy(from_left, step - 1, c, 0).wait_recv()

                @pl.when(can_right)
                def _():
                    line_copy(from_left, step, c, 0).start()

            @pl.when(from_right < LINE)
            def _():
                line_copy(from_right, step - 1, c, 1).wait_recv()

                @pl.when(can_left)
                def _():
                    line_copy(from_right, step, c, 1).start()

        @pl.when(from_left >= 0)
        def _():
            select(from_left, all_ref.at[from_left])

        @pl.when(from_right < LINE)
        def _():
            select(from_right, all_ref.at[from_right])

        return 0

    lax.fori_loop(1, LINE, advance, 0)
    if after is not None:
        after()

    def drain(step, _):
        for c in range(2):
            @pl.when(jnp.logical_and(z - step >= 0, can_right))
            def _():
                line_copy(z - step, step, c, 0).wait_send()

            @pl.when(jnp.logical_and(z + step < LINE, can_left))
            def _():
                line_copy(z + step, step, c, 1).wait_send()

        for e in range(1, PLANE):
            plane_copy(step, e).wait()
        return 0

    lax.fori_loop(0, LINE, drain, 0)
    swap = swap_matrix()
    for source in range(PLANE):
        block = jnp.dot(
            swap, got[source].reshape(BS, features), preferred_element_type=jnp.float32
        ).astype(jnp.bfloat16)
        out_ref[:, source] = block.reshape(8, 16, features)


def collect(terms_ref, act_ref, pos_ref, res_ref, stage, got, sums, from_left, from_right, right_sum,
            left_sum, line_sems, plane_sems, place):
    z, q = place
    features = act_ref.shape[1]
    swap = swap_matrix()
    for e in range(PLANE):
        to = (q + e) % PLANE
        block = jnp.dot(
            swap, terms_ref[:, to].reshape(BS, features), preferred_element_type=jnp.float32
        ).astype(jnp.bfloat16)
        if e == 0:
            got[q] = block.reshape(LINE, 16, features)
        else:
            stage[to] = block.reshape(LINE, 16, features)

    def plane_copy(d, e):
        to = (q + e) % PLANE
        return lat_copy(
            stage.at[to, d], got.at[q, d], plane_sems.at[0, d, e - 1], plane_sems.at[1, d, e - 1], z, to
        )

    def line_copy(d, far, c, way):
        land = from_right if way else from_left
        return lat_copy(
            sums.at[d, :, half(c, features)],
            land.at[d, :, half(c, features)],
            line_sems.at[0, way, far, c],
            line_sems.at[1, way, far, c],
            z + 1 - 2 * way,
            q,
        )

    def send_out(i, _):
        far = LINE - 1 - i

        @pl.when(z + far < LINE)
        def _():
            for e in range(1, PLANE):
                plane_copy(z + far, e).start()

        @pl.when(jnp.logical_and(z - far >= 0, far > 0))
        def _():
            for e in range(1, PLANE):
                plane_copy(z - far, e).start()

        return 0

    lax.fori_loop(0, LINE, send_out, 0)

    def partial(d):
        for e in range(1, PLANE):
            plane_copy(d, e).wait_recv()
        hit = slot_matrix(pos_ref[d]).astype(jnp.bfloat16)
        terms = got[:, d].reshape(BS, features)
        return lax.dot_general(
            hit, terms, (((0,), (0,)), ((), ())), preferred_element_type=jnp.float32
        )

    def advance(i, _):
        far = LINE - 1 - i
        right, left = z + far, z - far
        go_right, go_left = right < LINE, left >= 0

        @pl.when(go_right)
        def _():
            right_sum[...] = partial(right)

        @pl.when(go_left)
        def _():
            left_sum[...] = partial(left)

        for c in range(2):
            part = half(c, features)

            @pl.when(go_right)
            def _():
                @pl.when(z > 0)
                def _():
                    line_copy(right, far + 1, c, 0).wait_recv()
                    right_sum[:, part] += from_left[right, :, part].astype(jnp.float32)

                sums[right, :, part] = right_sum[:, part].astype(jnp.bfloat16)
                line_copy(right, far, c, 0).start()

            @pl.when(go_left)
            def _():
                @pl.when(z < LINE - 1)
                def _():
                    line_copy(left, far + 1, c, 1).wait_recv()
                    left_sum[:, part] += from_right[left, :, part].astype(jnp.float32)

                sums[left, :, part] = left_sum[:, part].astype(jnp.bfloat16)
                line_copy(left, far, c, 1).start()

        return 0

    lax.fori_loop(0, LINE - 1, advance, 0)
    right_sum[...] = partial(z) - act_ref[...].astype(jnp.float32)

    @pl.when(z > 0)
    def _():
        for c in range(2):
            line_copy(z, 1, c, 0).wait_recv()
        right_sum[...] += from_left[z].astype(jnp.float32)

    @pl.when(z < LINE - 1)
    def _():
        for c in range(2):
            line_copy(z, 1, c, 1).wait_recv()
        right_sum[...] += from_right[z].astype(jnp.float32)

    res_ref[...] = right_sum[...].astype(jnp.bfloat16)

    def drain(far, _):
        for c in range(2):
            @pl.when(jnp.logical_and(z + far < LINE, far > 0))
            def _():
                line_copy(z + far, far, c, 0).wait_send()

            @pl.when(jnp.logical_and(z - far >= 0, far > 0))
            def _():
                line_copy(z - far, far, c, 1).wait_send()

        for e in range(1, PLANE):
            plane_copy(far, e).wait_send()
        return 0

    return drain


def column(row):
    r = lax.broadcasted_iota(jnp.int32, (BS, BS), 0)
    col = lax.broadcasted_iota(jnp.int32, (BS, BS), 1)
    return jnp.sum(jnp.where(r == col, row, 0.0), axis=1, keepdims=True)


def flat_row(values):
    r = lax.broadcasted_iota(jnp.int32, (BS, BS), 0)
    col = lax.broadcasted_iota(jnp.int32, (BS, BS), 1)
    return jnp.sum(jnp.where(r == col, values, 0.0), axis=0, keepdims=True)


def step_kernel(x_ref, bias_ref, enc_ref, dec_ref,
                in_ref, dpre_ref, grad_ref, small_ref,
                all_a, stage_a, got_a, line_a, plane_a,
                sq_ref, sq_y, sq_mine, sq_z,
                codes_ref, unit_ref, row_ref, resid_ref, raw_ref, scaled_ref,
                part_b, got_yb, mine_b, got_zb, pre_ref, sems_b,
                terms_ref, res_ref, stage_c, got_c, sums, from_left, from_right, right_sum, left_sum,
                line_c, plane_c,
                all_d, stage_d, got_d, line_d, plane_d,
                part_e, got_ye, mine_e, got_ze, sems_e, pos_ref):
    place = lat_place()
    wid = wid_place()
    hi, y, partner, peers = wid
    rows = BS
    features = x_ref.shape[1]
    f32, bf16 = jnp.float32, jnp.bfloat16
    greet(place, wid)

    def sq_copy(d):
        return pltpu.make_async_remote_copy(
            src_ref=sq_ref, dst_ref=sq_y.at[d - 1], send_sem=sems_b.at[0, 13 + d],
            recv_sem=sems_b.at[1, 13 + d], device_id={"wid": peers[d - 1]}, device_id_type=MESH,
        )

    sq_far = pltpu.make_async_remote_copy(
        src_ref=sq_mine, dst_ref=sq_z, send_sem=sems_b.at[0, 17], recv_sem=sems_b.at[1, 17],
        device_id={"wid": partner}, device_id_type=MESH,
    )

    def square():
        for k in range(8):
            wide = dec_ref[k].astype(f32)
            total = jnp.sum(wide * wide, axis=1, keepdims=True)
            sq_ref[k : k + 1, :] = flat_row(total)
        for d in (1, 2, 3):
            sq_copy(d).start()

    def sum_squares():
        for d in (1, 2, 3):
            sq_copy(d).wait()
        sq_mine[...] = sq_ref[...] + sq_y[0] + sq_y[1] + sq_y[2]
        sq_far.start()

    spread(x_ref, all_a, pos_ref, stage_a, got_a, in_ref, line_a, plane_a, place, True, square, sum_squares)

    for k in range(8):
        part_b[k // 4, k % 4] = jnp.dot(
            in_ref[k].reshape(BS, features), enc_ref[:, k * BS : (k + 1) * BS], preferred_element_type=f32
        ).astype(bf16)

    def normalize():
        sq_far.wait()
        row_ref[...] = jnp.sqrt(sq_mine[...] + sq_z[...] + EPS)
        for k in range(8):
            norm = column(row_ref[k : k + 1, :])
            unit = (dec_ref[k].astype(f32) / norm).astype(bf16)
            unit_ref[k] = unit
            scaled_ref[k] = unit.astype(f32) / norm

    def live(h):
        return in_ref[h * 4 + y].reshape(BS, features)[:, 0:1].astype(f32) < 1.5

    def encode(h, total):
        preact = total + bias_ref[h * 4 + y]
        pre_ref[h] = preact
        codes_ref[h, y] = jnp.where(live(h), gelu(preact), 0.0).astype(bf16)
        return hand_on(codes_ref.at[h, y], sems_b, 7 + 3 * h, wid)

    wid_sum(part_b, got_yb, mine_b, got_zb, sems_b, wid, normalize, encode)

    for k in range(8):
        terms_ref[k] = (
            jnp.dot(codes_ref[k // 4, k % 4], unit_ref[k], preferred_element_type=f32)
            .astype(bf16)
            .reshape(PLANE, 16, features)
        )
    drain = collect(terms_ref, x_ref.at[0:rows, :], pos_ref, res_ref, stage_c, got_c, sums, from_left,
                    from_right, right_sum, left_sum, line_c, plane_c, place)
    spread(res_ref, all_d, pos_ref, stage_d, got_d, resid_ref, line_d, plane_d, place, False)

    for k in range(8):
        part_e[k // 4, k % 4] = lax.dot_general(
            resid_ref[k].reshape(BS, features), unit_ref[k], (((1,), (1,)), ((), ())),
            preferred_element_type=f32,
        ).astype(bf16)

    def decoder_sums():
        for k in range(8):
            raw = lax.dot_general(
                codes_ref[k // 4, k % 4], resid_ref[k].reshape(BS, features), (((0,), (0,)), ((), ())),
                preferred_element_type=f32,
            )
            raw_ref[k] = raw / column(row_ref[k : k + 1, :])
        lax.fori_loop(0, LINE, drain, 0)

    def differentiate(h, dcode):
        dpre = jnp.where(live(h), dcode * gelu_slope(pre_ref[h]), 0.0)
        dpre_ref[h, y] = dpre.astype(bf16)
        along = jnp.sum(codes_ref[h, y].astype(f32) * dcode, axis=0, keepdims=True)
        bias_grad = jnp.sum(dpre, axis=0, keepdims=True)
        row = lax.broadcasted_iota(jnp.int32, (8, BS), 0)
        small_ref[h, y] = jnp.where(row == 0, along, bias_grad)
        return hand_on(dpre_ref.at[h, y], sems_e, 7 + 3 * h, wid) + hand_on(
            small_ref.at[h, y], sems_e, 13 + 3 * h, wid
        )

    wid_sum(part_e, got_ye, mine_e, got_ze, sems_e, wid, decoder_sums, differentiate)
    for k in range(8):
        along = column(small_ref[k // 4, k % 4, 0:1, :])
        grad_ref[k] = (raw_ref[k] - along * scaled_ref[k]).astype(bf16)


def slots_buffer(features):
    return pltpu.VMEM((8, 8, 16, features), jnp.bfloat16)


def lat_sems():
    return [pltpu.SemaphoreType.DMA((2, 2, LINE, 2)), pltpu.SemaphoreType.DMA((2, LINE, PLANE - 1))]


def run_step(x, bias, encoder, decoder):
    rows, features = BS, x.shape[1]
    f32, bf16 = jnp.float32, jnp.bfloat16
    slots = 2 * LINE * PLANE
    row_blocks = pltpu.VMEM((LINE, rows, features), bf16)
    slot = slots_buffer(features)
    wid_part = pltpu.VMEM((2, 4, slots, BS), bf16)
    sq_block = pltpu.VMEM((8, BS), f32)
    row_total = pltpu.VMEM((rows, features), f32)
    latents = pltpu.VMEM((8, BS, features), f32)
    return pl.pallas_call(
        step_kernel,
        out_shape=(
            jax.ShapeDtypeStruct((8, PLANE, 16, features), bf16),
            jax.ShapeDtypeStruct((2, 4, slots, BS), bf16),
            jax.ShapeDtypeStruct((8, BS, features), bf16),
            jax.ShapeDtypeStruct((2, 4, 8, BS), f32),
        ),
        in_specs=vmem(4),
        out_specs=tuple(vmem(4)),
        scratch_shapes=[pltpu.VMEM((LINE, x.shape[0], features), bf16), slot, slot]
        + lat_sems()
        + [sq_block, pltpu.VMEM((3, 8, BS), f32), sq_block, sq_block]
        + [wid_part, pltpu.VMEM((8, BS, features), bf16), sq_block, slot, latents, latents]
        + [wid_part]
        + sum_scratch(slots)
        + [pltpu.VMEM((2, slots, BS), f32), pltpu.SemaphoreType.DMA((2, 18))]
        + [slot, pltpu.VMEM((rows, features), bf16), slot, slot]
        + [row_blocks, row_blocks, row_blocks, row_total, row_total]
        + lat_sems()
        + [row_blocks, slot, slot]
        + lat_sems()
        + [wid_part]
        + sum_scratch(slots)
        + [pltpu.SemaphoreType.DMA((2, 20)), pltpu.VMEM((LINE, 8, BS), f32)],
        compiler_params=pltpu.CompilerParams(collective_id=0, has_side_effects=True),
        name="step",
    )(x, bias, encoder, decoder)


def body(activations, block_ids, alive_tallies, encoder, encoder_bias, decoder):
    rows, features = activations.shape
    slots = block_ids.shape[1]
    lat = lax.axis_size("lat")
    f32 = jnp.float32

    flat = block_ids.reshape(rows * slots)
    order = jnp.arange(rows * slots, dtype=jnp.int32)
    earlier = (flat[:, None] == flat[None, :]) & (order[None, :] < order[:, None])
    rank = jnp.sum(earlier.astype(jnp.int32), axis=1).reshape(rows, slots)
    alive = jnp.arange(slots, dtype=jnp.int32)[None, :] < alive_tallies[:, None]
    position = block_ids * 2 + rank
    high = jnp.where(alive, position >> 3, 255)
    codes_of_rows = jnp.concatenate([high, position & 7], axis=1).T.astype(jnp.bfloat16)
    extra = jnp.pad(codes_of_rows, ((0, 8), (0, features - rows)))
    incoming, dpre, decoder_grad, small = run_step(
        jnp.concatenate([activations, extra], axis=0),
        encoder_bias.reshape(8, 1, BS),
        encoder,
        decoder.reshape(8, BS, features),
    )
    incoming = incoming.reshape(8, lat * 2, features)
    dpre = dpre.reshape(8, lat * 2, BS)
    decoder_grad = decoder_grad.reshape(8 * BS, features)
    bias_grad = small.reshape(8, 8, BS)[:, 1].reshape(8 * BS)
    encoder_grad = (
        jnp.einsum("kiy,kif->ykf", incoming, dpre, preferred_element_type=f32)
        .reshape(features, 8 * BS)
        .astype(jnp.bfloat16)
    )
    return encoder_grad, decoder_grad, bias_grad


def solution(mesh):
    return jax.shard_map(
        body,
        mesh=mesh,
        in_specs=(
            P("lat", "wid"),
            P("lat", None),
            P("lat"),
            P("wid", "lat"),
            P("lat"),
            P("lat", "wid"),
        ),
        out_specs=(P("wid", "lat"), P("lat", "wid"), P("lat")),
        check_vma=False,
    )
```

```python
import jax
import jax.numpy as jnp
from jax import lax
from jax.experimental import pallas as pl
from jax.experimental.pallas import tpu as pltpu
from jax.sharding import PartitionSpec as P

BS = 128
EPS = 1e-06
C0 = 0.7978845608
C1 = 0.044715
FILLER = 2.0
LINE = 8
PLANE = 8
PIECES = 4
MESH = pl.DeviceIdType.MESH


def gelu(v):
    return 0.5 * v * (1.0 + jnp.tanh(C0 * (v + C1 * v * v * v)))


def gelu_slope(v):
    t = jnp.tanh(C0 * (v + C1 * v * v * v))
    return 0.5 * (1.0 + t) + 0.5 * v * (1.0 - t * t) * C0 * (1.0 + 3.0 * C1 * v * v)


def wid_place():
    me = lax.axis_index("wid")
    hi, y = me // 4, me % 4
    partner = (1 - hi) * 4 + y
    peers = [hi * 4 + (y + d) % 4 for d in (1, 2, 3)]
    return hi, y, partner, peers


def send(src, dst, send_sem, recv_sem, to):
    copy = pltpu.make_async_remote_copy(
        src_ref=src,
        dst_ref=dst,
        send_sem=send_sem,
        recv_sem=recv_sem,
        device_id={"wid": to},
        device_id_type=MESH,
    )
    copy.start()
    return copy


def wid_sum(part_ref, got_y, mine, got_z, sems, place, meanwhile, finish):
    hi, y, partner, peers = place
    near = [
        [
            send(part_ref.at[h, (y + d) % 4], got_y.at[d - 1, h], sems.at[0, 3 * h + d - 1],
                 sems.at[1, 3 * h + d - 1], peers[d - 1])
            for d in (1, 2, 3)
        ]
        for h in range(2)
    ]
    far = []
    for h in range(2):
        for copy in near[h]:
            copy.wait()
        s = part_ref[h, y].astype(jnp.float32)
        for d in range(3):
            s = s + got_y[d, h].astype(jnp.float32)
        mine[h] = s.astype(mine.dtype)
        far.append(send(mine.at[h], got_z.at[h], sems.at[0, 6 + h], sems.at[1, 6 + h], partner))
    meanwhile()
    late = []
    for h in range(2):
        far[h].wait()
        late += finish(h, mine[h].astype(jnp.float32) + got_z[h].astype(jnp.float32))
    for copy in late:
        copy.wait()


def hand_on(block, sems, base, place):
    peers = place[3]
    return [
        send(block, block, sems.at[0, base + d], sems.at[1, base + d], peers[d - 1]) for d in (1, 2, 3)
    ]


def vmem(n):
    return [pl.BlockSpec(memory_space=pltpu.VMEM)] * n


def sum_scratch(slots):
    return [
        pltpu.VMEM((3, 2, slots, BS), jnp.bfloat16),
        pltpu.VMEM((2, slots, BS), jnp.bfloat16),
        pltpu.VMEM((2, slots, BS), jnp.bfloat16),
    ]


def lat_place():
    me = lax.axis_index("lat")
    return me // PLANE, me % PLANE


def greet(place, wid):
    z, q = place
    _, _, partner, peers = wid
    barrier = pltpu.get_barrier_semaphore()

    def signal(**other):
        pl.semaphore_signal(barrier, inc=1, device_id=other, device_id_type=MESH)

    for other in [partner] + peers:
        signal(wid=other)
    for e in range(1, PLANE):
        signal(lat=z * PLANE + (q + e) % PLANE)

    @pl.when(z > 0)
    def _():
        signal(lat=(z - 1) * PLANE + q)

    @pl.when(z < LINE - 1)
    def _():
        signal(lat=(z + 1) * PLANE + q)

    inner = jnp.logical_and(z > 0, z < LINE - 1)

    @pl.when(inner)
    def _():
        pl.semaphore_wait(barrier, PLANE + 5)

    @pl.when(jnp.logical_not(inner))
    def _():
        pl.semaphore_wait(barrier, PLANE + 4)


def lat_copy(src, dst, send_sem, recv_sem, z, q):
    return pltpu.make_async_remote_copy(
        src_ref=src,
        dst_ref=dst,
        send_sem=send_sem,
        recv_sem=recv_sem,
        device_id={"lat": z * PLANE + q},
        device_id_type=MESH,
    )


def piece(c):
    return pl.ds(c * (BS // PIECES), BS // PIECES)


def slot_matrix(local):
    spots = lax.broadcasted_iota(jnp.int32, (BS, BS), 0).astype(jnp.float32)
    hit = jnp.zeros((BS, BS), jnp.float32)
    for j in range(4):
        hit = hit + jnp.where(spots == local[j : j + 1, :], 1.0, 0.0)
    return hit


def swap_matrix():
    r = lax.broadcasted_iota(jnp.int32, (BS, BS), 0)
    col = lax.broadcasted_iota(jnp.int32, (BS, BS), 1)
    source = ((r >> 1) & 7) * 16 + (r >> 4) * 2 + (r & 1)
    return jnp.where(source == col, 1.0, 0.0).astype(jnp.bfloat16)


def spread(x_ref, all_ref, pos_ref, stage, got, out_ref, line_sems, plane_sems, place, own_code=None,
           code_ref=None, meanwhile=None, after=None):
    z, q = place
    features = x_ref.shape[1]
    first = own_code is not None
    pieces = PIECES + first

    def line_copy(b, step, c, way, own=False):
        if first and c == 0:
            src, dst = own_code if own else code_ref.at[b], code_ref.at[b]
        else:
            part = piece(c - first)
            src = x_ref.at[part] if own else all_ref.at[b, part]
            dst = all_ref.at[b, part]
        return lat_copy(
            src,
            dst,
            line_sems.at[0, way, step, c],
            line_sems.at[1, way, step, c],
            z + 1 - 2 * way,
            q,
        )

    def plane_copy(b, e):
        to = (q + e) % PLANE
        return lat_copy(
            stage.at[b, to], got.at[q, b], plane_sems.at[0, b, e - 1], plane_sems.at[1, b, e - 1], z, to
        )

    def select(b, ref, codes):
        if first:
            code = codes[0:8, :].astype(jnp.float32)
            base = (z * BS).astype(jnp.float32)
            local = code[0:4] * 8.0 + code[4:8] - base
            pos_ref[b] = jnp.concatenate([local, local], axis=0)
        else:
            local = pos_ref[b]
        hit = slot_matrix(local)
        picked = jnp.dot(hit.astype(jnp.bfloat16), ref[...], preferred_element_type=jnp.float32)
        if first:
            filled = jnp.sum(hit, axis=1, keepdims=True)
            picked = jnp.where(filled > 0.5, picked, FILLER)
        stage[b] = picked.astype(jnp.bfloat16).reshape(PLANE, 16, features)
        got[q, b] = stage[b, q]
        for e in range(1, PLANE):
            plane_copy(b, e).start()

    can_right, can_left = z < LINE - 1, z > 0
    for c in range(pieces):
        @pl.when(can_right)
        def _():
            line_copy(z, 0, c, 0, True).start()

        @pl.when(can_left)
        def _():
            line_copy(z, 0, c, 1, True).start()

    select(z, x_ref, own_code)
    if meanwhile is not None:
        meanwhile()

    def advance(step, _):
        from_left, from_right = z - step, z + step
        for c in range(pieces):
            @pl.when(from_left >= 0)
            def _():
                line_copy(from_left, step - 1, c, 0).wait_recv()

                @pl.when(can_right)
                def _():
                    line_copy(from_left, step, c, 0).start()

            @pl.when(from_right < LINE)
            def _():
                line_copy(from_right, step - 1, c, 1).wait_recv()

                @pl.when(can_left)
                def _():
                    line_copy(from_right, step, c, 1).start()

        @pl.when(from_left >= 0)
        def _():
            select(from_left, all_ref.at[from_left], code_ref.at[from_left] if first else None)

        @pl.when(from_right < LINE)
        def _():
            select(from_right, all_ref.at[from_right], code_ref.at[from_right] if first else None)

        return 0

    lax.fori_loop(1, LINE, advance, 0)
    if after is not None:
        after()

    def drain(step, _):
        for c in range(pieces):
            @pl.when(jnp.logical_and(z - step >= 0, can_right))
            def _():
                line_copy(z - step, step, c, 0).wait_send()

            @pl.when(jnp.logical_and(z + step < LINE, can_left))
            def _():
                line_copy(z + step, step, c, 1).wait_send()

        for e in range(1, PLANE):
            plane_copy(step, e).wait()
        return 0

    lax.fori_loop(0, LINE, drain, 0)
    swap = swap_matrix()
    for source in range(PLANE):
        block = jnp.dot(
            swap, got[source].reshape(BS, features), preferred_element_type=jnp.float32
        ).astype(jnp.bfloat16)
        out_ref[:, source] = block.reshape(8, 16, features)


def collect(terms_ref, act_ref, pos_ref, res_ref, stage, got, sums, from_left, from_right, right_sum,
            left_sum, line_sems, plane_sems, place):
    z, q = place
    features = act_ref.shape[1]
    swap = swap_matrix()
    for e in range(PLANE):
        to = (q + e) % PLANE
        block = jnp.dot(
            swap, terms_ref[:, to].reshape(BS, features), preferred_element_type=jnp.float32
        ).astype(jnp.bfloat16)
        if e == 0:
            got[q] = block.reshape(LINE, 16, features)
        else:
            stage[to] = block.reshape(LINE, 16, features)

    def plane_copy(d, e):
        to = (q + e) % PLANE
        return lat_copy(
            stage.at[to, d], got.at[q, d], plane_sems.at[0, d, e - 1], plane_sems.at[1, d, e - 1], z, to
        )

    def line_copy(d, far, c, way):
        land = from_right if way else from_left
        return lat_copy(
            sums.at[d, piece(c)],
            land.at[d, piece(c)],
            line_sems.at[0, way, far, c],
            line_sems.at[1, way, far, c],
            z + 1 - 2 * way,
            q,
        )

    def send_out(i, _):
        far = LINE - 1 - i

        @pl.when(z + far < LINE)
        def _():
            for e in range(1, PLANE):
                plane_copy(z + far, e).start()

        @pl.when(jnp.logical_and(z - far >= 0, far > 0))
        def _():
            for e in range(1, PLANE):
                plane_copy(z - far, e).start()

        return 0

    lax.fori_loop(0, LINE, send_out, 0)

    def partial(d):
        for e in range(1, PLANE):
            plane_copy(d, e).wait_recv()
        hit = slot_matrix(pos_ref[d]).astype(jnp.bfloat16)
        terms = got[:, d].reshape(BS, features)
        return lax.dot_general(
            hit, terms, (((0,), (0,)), ((), ())), preferred_element_type=jnp.float32
        )

    def advance(i, _):
        far = LINE - 1 - i
        right, left = z + far, z - far
        go_right, go_left = right < LINE, left >= 0

        @pl.when(go_right)
        def _():
            right_sum[...] = partial(right)

        @pl.when(go_left)
        def _():
            left_sum[...] = partial(left)

        for c in range(PIECES):
            part = piece(c)

            @pl.when(go_right)
            def _():
                @pl.when(z > 0)
                def _():
                    line_copy(right, far + 1, c, 0).wait_recv()
                    right_sum[part, :] += from_left[right, part, :].astype(jnp.float32)

                sums[right, part, :] = right_sum[part, :].astype(jnp.bfloat16)
                line_copy(right, far, c, 0).start()

            @pl.when(go_left)
            def _():
                @pl.when(z < LINE - 1)
                def _():
                    line_copy(left, far + 1, c, 1).wait_recv()
                    left_sum[part, :] += from_right[left, part, :].astype(jnp.float32)

                sums[left, part, :] = left_sum[part, :].astype(jnp.bfloat16)
                line_copy(left, far, c, 1).start()

        return 0

    lax.fori_loop(0, LINE - 1, advance, 0)
    right_sum[...] = partial(z) - act_ref[...].astype(jnp.float32)

    @pl.when(z > 0)
    def _():
        for c in range(PIECES):
            line_copy(z, 1, c, 0).wait_recv()
        right_sum[...] += from_left[z].astype(jnp.float32)

    @pl.when(z < LINE - 1)
    def _():
        for c in range(PIECES):
            line_copy(z, 1, c, 1).wait_recv()
        right_sum[...] += from_right[z].astype(jnp.float32)

    res_ref[...] = right_sum[...].astype(jnp.bfloat16)

    def drain(far, _):
        for c in range(PIECES):
            @pl.when(jnp.logical_and(z + far < LINE, far > 0))
            def _():
                line_copy(z + far, far, c, 0).wait_send()

            @pl.when(jnp.logical_and(z - far >= 0, far > 0))
            def _():
                line_copy(z - far, far, c, 1).wait_send()

        for e in range(1, PLANE):
            plane_copy(far, e).wait_send()
        return 0

    return drain


def column(row):
    r = lax.broadcasted_iota(jnp.int32, (BS, BS), 0)
    col = lax.broadcasted_iota(jnp.int32, (BS, BS), 1)
    return jnp.sum(jnp.where(r == col, row, 0.0), axis=1, keepdims=True)


def flat_row(values):
    r = lax.broadcasted_iota(jnp.int32, (BS, BS), 0)
    col = lax.broadcasted_iota(jnp.int32, (BS, BS), 1)
    return jnp.sum(jnp.where(r == col, values, 0.0), axis=0, keepdims=True)


def step_kernel(x_ref, code_ref, bias_ref, enc_ref, dec_ref,
                enc_grad_ref, grad_ref, bias_grad_ref,
                in_ref, turned_ref, dpre_ref, small_ref, all_a, code_all, stage_a, got_a, line_a, plane_a,
                sq_ref, sq_y, sq_mine, sq_z,
                codes_ref, unit_ref, row_ref, resid_ref, raw_ref, scaled_ref,
                part_b, got_yb, mine_b, got_zb, pre_ref, sems_b,
                terms_ref, res_ref, stage_c, got_c, sums, from_left, from_right, right_sum, left_sum,
                line_c, plane_c,
                all_d, stage_d, got_d, line_d, plane_d,
                part_e, got_ye, mine_e, got_ze, sems_e, pos_ref):
    place = lat_place()
    wid = wid_place()
    hi, y, partner, peers = wid
    features = x_ref.shape[1]
    f32, bf16 = jnp.float32, jnp.bfloat16
    greet(place, wid)

    def sq_copy(d):
        return pltpu.make_async_remote_copy(
            src_ref=sq_ref, dst_ref=sq_y.at[d - 1], send_sem=sems_b.at[0, 13 + d],
            recv_sem=sems_b.at[1, 13 + d], device_id={"wid": peers[d - 1]}, device_id_type=MESH,
        )

    sq_far = pltpu.make_async_remote_copy(
        src_ref=sq_mine, dst_ref=sq_z, send_sem=sems_b.at[0, 17], recv_sem=sems_b.at[1, 17],
        device_id={"wid": partner}, device_id_type=MESH,
    )

    def square():
        for k in range(8):
            wide = dec_ref[k].astype(f32)
            total = jnp.sum(wide * wide, axis=1, keepdims=True)
            sq_ref[k : k + 1, :] = flat_row(total)
        for d in (1, 2, 3):
            sq_copy(d).start()

    def sum_squares():
        for d in (1, 2, 3):
            sq_copy(d).wait()
        sq_mine[...] = sq_ref[...] + sq_y[0] + sq_y[1] + sq_y[2]
        sq_far.start()

    spread(x_ref, all_a, pos_ref, stage_a, got_a, in_ref, line_a, plane_a, place, code_ref, code_all,
           square, sum_squares)

    for k in range(8):
        part_b[k // 4, k % 4] = jnp.dot(
            in_ref[k].reshape(BS, features), enc_ref[:, k * BS : (k + 1) * BS], preferred_element_type=f32
        ).astype(bf16)

    def normalize():
        sq_far.wait()
        row_ref[...] = jnp.sqrt(sq_mine[...] + sq_z[...] + EPS)
        for k in range(8):
            norm = column(row_ref[k : k + 1, :])
            unit = (dec_ref[k].astype(f32) / norm).astype(bf16)
            unit_ref[k] = unit
            scaled_ref[k] = unit.astype(f32) / norm

    def live(h):
        return in_ref[h * 4 + y].reshape(BS, features)[:, 0:1].astype(f32) < 1.5

    def encode(h, total):
        preact = total + bias_ref[h * 4 + y]
        pre_ref[h] = preact
        codes_ref[h, y] = jnp.where(live(h), gelu(preact), 0.0).astype(bf16)
        return hand_on(codes_ref.at[h, y], sems_b, 7 + 3 * h, wid)

    wid_sum(part_b, got_yb, mine_b, got_zb, sems_b, wid, normalize, encode)

    for k in range(8):
        terms_ref[k] = (
            jnp.dot(codes_ref[k // 4, k % 4], unit_ref[k], preferred_element_type=f32)
            .astype(bf16)
            .reshape(PLANE, 16, features)
        )
    drain = collect(terms_ref, x_ref, pos_ref, res_ref, stage_c, got_c, sums, from_left,
                    from_right, right_sum, left_sum, line_c, plane_c, place)
    spread(res_ref, all_d, pos_ref, stage_d, got_d, resid_ref, line_d, plane_d, place)

    for k in range(8):
        part_e[k // 4, k % 4] = lax.dot_general(
            resid_ref[k].reshape(BS, features), unit_ref[k], (((1,), (1,)), ((), ())),
            preferred_element_type=f32,
        ).astype(bf16)

    def decoder_sums():
        for k in range(8):
            raw = lax.dot_general(
                codes_ref[k // 4, k % 4], resid_ref[k].reshape(BS, features), (((0,), (0,)), ((), ())),
                preferred_element_type=f32,
            )
            raw_ref[k] = raw / column(row_ref[k : k + 1, :])
            turned_ref[k] = in_ref[k].reshape(BS, features).T
        lax.fori_loop(0, LINE, drain, 0)

    def differentiate(h, dcode):
        dpre = jnp.where(live(h), dcode * gelu_slope(pre_ref[h]), 0.0)
        dpre_ref[h, y] = dpre.astype(bf16)
        along = jnp.sum(codes_ref[h, y].astype(f32) * dcode, axis=0, keepdims=True)
        bias_grad = jnp.sum(dpre, axis=0, keepdims=True)
        row = lax.broadcasted_iota(jnp.int32, (8, BS), 0)
        small_ref[h, y] = jnp.where(row == 0, along, bias_grad)
        return hand_on(dpre_ref.at[h, y], sems_e, 7 + 3 * h, wid) + hand_on(
            small_ref.at[h, y], sems_e, 13 + 3 * h, wid
        )

    wid_sum(part_e, got_ye, mine_e, got_ze, sems_e, wid, decoder_sums, differentiate)
    for k in range(8):
        enc_grad_ref[:, k * BS : (k + 1) * BS] = jnp.dot(
            turned_ref[k], dpre_ref[k // 4, k % 4], preferred_element_type=f32
        ).astype(bf16)
        bias_grad_ref[k : k + 1, :] = small_ref[k // 4, k % 4, 1:2, :]
        along = column(small_ref[k // 4, k % 4, 0:1, :])
        grad_ref[k] = (raw_ref[k] - along * scaled_ref[k]).astype(bf16)


def slots_buffer(features):
    return pltpu.VMEM((8, 8, 16, features), jnp.bfloat16)


def lat_sems():
    return [pltpu.SemaphoreType.DMA((2, 2, LINE, PIECES + 1)), pltpu.SemaphoreType.DMA((2, LINE, PLANE - 1))]


def run_step(x, codes, bias, encoder, decoder):
    rows, features = BS, x.shape[1]
    f32, bf16 = jnp.float32, jnp.bfloat16
    slots = 2 * LINE * PLANE
    row_blocks = pltpu.VMEM((LINE, rows, features), bf16)
    slot = slots_buffer(features)
    wid_part = pltpu.VMEM((2, 4, slots, BS), bf16)
    sq_block = pltpu.VMEM((8, BS), f32)
    row_total = pltpu.VMEM((rows, features), f32)
    latents = pltpu.VMEM((8, BS, features), f32)
    return pl.pallas_call(
        step_kernel,
        out_shape=(
            jax.ShapeDtypeStruct((features, 8 * BS), bf16),
            jax.ShapeDtypeStruct((8, BS, features), bf16),
            jax.ShapeDtypeStruct((8, BS), f32),
        ),
        in_specs=vmem(5),
        out_specs=tuple(vmem(3)),
        scratch_shapes=[slot, pltpu.VMEM((8, features, BS), bf16), wid_part]
        + [pltpu.VMEM((2, 4, 8, BS), f32)]
        + [row_blocks, pltpu.VMEM((LINE, 16, BS), bf16), slot, slot]
        + lat_sems()
        + [sq_block, pltpu.VMEM((3, 8, BS), f32), sq_block, sq_block]
        + [wid_part, pltpu.VMEM((8, BS, features), bf16), sq_block, slot, latents, latents]
        + [wid_part]
        + sum_scratch(slots)
        + [pltpu.VMEM((2, slots, BS), f32), pltpu.SemaphoreType.DMA((2, 18))]
        + [slot, pltpu.VMEM((rows, features), bf16), slot, slot]
        + [row_blocks, row_blocks, row_blocks, row_total, row_total]
        + lat_sems()
        + [row_blocks, slot, slot]
        + lat_sems()
        + [wid_part]
        + sum_scratch(slots)
        + [pltpu.SemaphoreType.DMA((2, 20)), pltpu.VMEM((LINE, 8, BS), f32)],
        compiler_params=pltpu.CompilerParams(collective_id=0, has_side_effects=True),
        name="step",
    )(x, codes, bias, encoder, decoder)


def body(activations, block_ids, alive_tallies, encoder, encoder_bias, decoder):
    rows, features = activations.shape
    slots = block_ids.shape[1]
    lat = lax.axis_size("lat")
    f32 = jnp.float32

    flat = block_ids.reshape(rows * slots)
    order = jnp.arange(rows * slots, dtype=jnp.int32)
    earlier = (flat[:, None] == flat[None, :]) & (order[None, :] < order[:, None])
    rank = jnp.sum(earlier.astype(jnp.int32), axis=1).reshape(rows, slots)
    alive = jnp.arange(slots, dtype=jnp.int32)[None, :] < alive_tallies[:, None]
    position = block_ids * 2 + rank
    high = jnp.where(alive, position >> 3, 255)
    codes_of_rows = jnp.concatenate([high, position & 7], axis=1).T.astype(jnp.bfloat16)
    extra = jnp.pad(codes_of_rows, ((0, 8), (0, 0)))
    encoder_grad, decoder_grad, bias_grad = run_step(
        activations, extra, encoder_bias.reshape(8, 1, BS), encoder, decoder.reshape(8, BS, features)
    )
    decoder_grad = decoder_grad.reshape(8 * BS, features)
    bias_grad = bias_grad.reshape(8 * BS)
    return encoder_grad, decoder_grad, bias_grad


def solution(mesh):
    return jax.shard_map(
        body,
        mesh=mesh,
        in_specs=(
            P("lat", "wid"),
            P("lat", None),
            P("lat"),
            P("wid", "lat"),
            P("lat"),
            P("lat", "wid"),
        ),
        out_specs=(P("wid", "lat"), P("lat", "wid"), P("lat")),
        check_vma=False,
    )
```

```python
import jax
import jax.numpy as jnp
from jax import lax
from jax.experimental import pallas as pl
from jax.experimental.pallas import tpu as pltpu
from jax.sharding import PartitionSpec as P

BS = 128
EPS = 1e-06
C0 = 0.7978845608
C1 = 0.044715
FILLER = 2.0
LINE = 8
PLANE = 8
PIECES = 4
MESH = pl.DeviceIdType.MESH


def gelu(v):
    return 0.5 * v * (1.0 + jnp.tanh(C0 * (v + C1 * v * v * v)))


def gelu_slope(v):
    t = jnp.tanh(C0 * (v + C1 * v * v * v))
    return 0.5 * (1.0 + t) + 0.5 * v * (1.0 - t * t) * C0 * (1.0 + 3.0 * C1 * v * v)


def wid_place():
    me = lax.axis_index("wid")
    hi, y = me // 4, me % 4
    partner = (1 - hi) * 4 + y
    peers = [hi * 4 + (y + d) % 4 for d in (1, 2, 3)]
    return hi, y, partner, peers


def send(src, dst, send_sem, recv_sem, to):
    copy = pltpu.make_async_remote_copy(
        src_ref=src,
        dst_ref=dst,
        send_sem=send_sem,
        recv_sem=recv_sem,
        device_id={"wid": to},
        device_id_type=MESH,
    )
    copy.start()
    return copy


def wid_sum(part_ref, got_y, mine, got_z, sems, place, fill, meanwhile, finish):
    hi, y, partner, peers = place
    near = []
    for h in range(2):
        fill(h)
        near.append([
            send(part_ref.at[h, (y + d) % 4], got_y.at[d - 1, h], sems.at[0, 3 * h + d - 1],
                 sems.at[1, 3 * h + d - 1], peers[d - 1])
            for d in (1, 2, 3)
        ])
    far = []
    for h in range(2):
        for copy in near[h]:
            copy.wait()
        s = part_ref[h, y].astype(jnp.float32)
        for d in range(3):
            s = s + got_y[d, h].astype(jnp.float32)
        mine[h] = s.astype(mine.dtype)
        far.append(send(mine.at[h], got_z.at[h], sems.at[0, 6 + h], sems.at[1, 6 + h], partner))
    meanwhile()
    late = []
    for h in range(2):
        far[h].wait()
        late += finish(h, mine[h].astype(jnp.float32) + got_z[h].astype(jnp.float32))
    for copy in late:
        copy.wait()


def hand_on(block, sems, base, place):
    peers = place[3]
    return [
        send(block, block, sems.at[0, base + d], sems.at[1, base + d], peers[d - 1]) for d in (1, 2, 3)
    ]


def vmem(n):
    return [pl.BlockSpec(memory_space=pltpu.VMEM)] * n


def sum_scratch(slots):
    return [
        pltpu.VMEM((3, 2, slots, BS), jnp.bfloat16),
        pltpu.VMEM((2, slots, BS), jnp.bfloat16),
        pltpu.VMEM((2, slots, BS), jnp.bfloat16),
    ]


def lat_place():
    me = lax.axis_index("lat")
    return me // PLANE, me % PLANE


def greet(place, wid):
    z, q = place
    _, _, partner, peers = wid
    barrier = pltpu.get_barrier_semaphore()

    def signal(**other):
        pl.semaphore_signal(barrier, inc=1, device_id=other, device_id_type=MESH)

    for other in [partner] + peers:
        signal(wid=other)
    for e in range(1, PLANE):
        signal(lat=z * PLANE + (q + e) % PLANE)

    @pl.when(z > 0)
    def _():
        signal(lat=(z - 1) * PLANE + q)

    @pl.when(z < LINE - 1)
    def _():
        signal(lat=(z + 1) * PLANE + q)

    inner = jnp.logical_and(z > 0, z < LINE - 1)

    @pl.when(inner)
    def _():
        pl.semaphore_wait(barrier, PLANE + 5)

    @pl.when(jnp.logical_not(inner))
    def _():
        pl.semaphore_wait(barrier, PLANE + 4)


def lat_copy(src, dst, send_sem, recv_sem, z, q):
    return pltpu.make_async_remote_copy(
        src_ref=src,
        dst_ref=dst,
        send_sem=send_sem,
        recv_sem=recv_sem,
        device_id={"lat": z * PLANE + q},
        device_id_type=MESH,
    )


def piece(c):
    return pl.ds(c * (BS // PIECES), BS // PIECES)


def slot_matrix(local):
    spots = lax.broadcasted_iota(jnp.int32, (BS, BS), 0).astype(jnp.float32)
    hit = jnp.zeros((BS, BS), jnp.float32)
    for j in range(4):
        hit = hit + jnp.where(spots == local[j : j + 1, :], 1.0, 0.0)
    return hit


def swap_matrix():
    r = lax.broadcasted_iota(jnp.int32, (BS, BS), 0)
    col = lax.broadcasted_iota(jnp.int32, (BS, BS), 1)
    source = ((r >> 1) & 7) * 16 + (r >> 4) * 2 + (r & 1)
    return jnp.where(source == col, 1.0, 0.0).astype(jnp.bfloat16)


def spread(x_ref, all_ref, pos_ref, stage, got, out_ref, line_sems, plane_sems, place, own_code=None,
           code_ref=None, meanwhile=None, after=None):
    z, q = place
    features = x_ref.shape[1]
    first = own_code is not None
    pieces = PIECES + first

    def line_copy(b, step, c, way, own=False):
        if first and c == 0:
            src, dst = own_code if own else code_ref.at[b], code_ref.at[b]
        else:
            part = piece(c - first)
            src = x_ref.at[part] if own else all_ref.at[b, part]
            dst = all_ref.at[b, part]
        return lat_copy(
            src,
            dst,
            line_sems.at[0, way, step, c],
            line_sems.at[1, way, step, c],
            z + 1 - 2 * way,
            q,
        )

    def plane_copy(b, e):
        to = (q + e) % PLANE
        return lat_copy(
            stage.at[b, to], got.at[q, b], plane_sems.at[0, b, e - 1], plane_sems.at[1, b, e - 1], z, to
        )

    def select(b, ref, codes):
        if first:
            code = codes[0:8, :].astype(jnp.float32)
            base = (z * BS).astype(jnp.float32)
            local = code[0:4] * 8.0 + code[4:8] - base
            pos_ref[b] = jnp.concatenate([local, local], axis=0)
        else:
            local = pos_ref[b]
        hit = slot_matrix(local)
        picked = jnp.dot(hit.astype(jnp.bfloat16), ref[...], preferred_element_type=jnp.float32)
        if first:
            filled = jnp.sum(hit, axis=1, keepdims=True)
            picked = jnp.where(filled > 0.5, picked, FILLER)
        stage[b] = picked.astype(jnp.bfloat16).reshape(PLANE, 16, features)
        got[q, b] = stage[b, q]
        for e in range(1, PLANE):
            plane_copy(b, e).start()

    can_right, can_left = z < LINE - 1, z > 0
    for c in range(pieces):
        @pl.when(can_right)
        def _():
            line_copy(z, 0, c, 0, True).start()

        @pl.when(can_left)
        def _():
            line_copy(z, 0, c, 1, True).start()

    select(z, x_ref, own_code)
    if meanwhile is not None:
        meanwhile()

    def advance(step, _):
        from_left, from_right = z - step, z + step
        for c in range(pieces):
            @pl.when(from_left >= 0)
            def _():
                line_copy(from_left, step - 1, c, 0).wait_recv()

                @pl.when(can_right)
                def _():
                    line_copy(from_left, step, c, 0).start()

            @pl.when(from_right < LINE)
            def _():
                line_copy(from_right, step - 1, c, 1).wait_recv()

                @pl.when(can_left)
                def _():
                    line_copy(from_right, step, c, 1).start()

        @pl.when(from_left >= 0)
        def _():
            select(from_left, all_ref.at[from_left], code_ref.at[from_left] if first else None)

        @pl.when(from_right < LINE)
        def _():
            select(from_right, all_ref.at[from_right], code_ref.at[from_right] if first else None)

        return 0

    lax.fori_loop(1, LINE, advance, 0)
    if after is not None:
        after()

    swap = swap_matrix()
    for e in range(PLANE):
        source = (q + PLANE - e) % PLANE
        if e > 0:
            for b in range(LINE):
                plane_copy(b, e).wait_recv()
        block = jnp.dot(
            swap, got[source].reshape(BS, features), preferred_element_type=jnp.float32
        ).astype(jnp.bfloat16)
        out_ref[:, source] = block.reshape(8, 16, features)

    def drain(step, _):
        for c in range(pieces):
            @pl.when(jnp.logical_and(z - step >= 0, can_right))
            def _():
                line_copy(z - step, step, c, 0).wait_send()

            @pl.when(jnp.logical_and(z + step < LINE, can_left))
            def _():
                line_copy(z + step, step, c, 1).wait_send()

        for e in range(1, PLANE):
            plane_copy(step, e).wait_send()
        return 0

    lax.fori_loop(0, LINE, drain, 0)


def collect(terms_ref, act_ref, pos_ref, res_ref, stage, got, sums, from_left, from_right, right_sum,
            left_sum, line_sems, plane_sems, place):
    z, q = place
    features = act_ref.shape[1]
    swap = swap_matrix()
    for e in range(PLANE):
        to = (q + e) % PLANE
        block = jnp.dot(
            swap, terms_ref[:, to].reshape(BS, features), preferred_element_type=jnp.float32
        ).astype(jnp.bfloat16)
        if e == 0:
            got[q] = block.reshape(LINE, 16, features)
        else:
            stage[to] = block.reshape(LINE, 16, features)

    def plane_copy(d, e):
        to = (q + e) % PLANE
        return lat_copy(
            stage.at[to, d], got.at[q, d], plane_sems.at[0, d, e - 1], plane_sems.at[1, d, e - 1], z, to
        )

    def line_copy(d, far, c, way):
        land = from_right if way else from_left
        return lat_copy(
            sums.at[d, piece(c)],
            land.at[d, piece(c)],
            line_sems.at[0, way, far, c],
            line_sems.at[1, way, far, c],
            z + 1 - 2 * way,
            q,
        )

    def send_out(i, _):
        far = LINE - 1 - i

        @pl.when(z + far < LINE)
        def _():
            for e in range(1, PLANE):
                plane_copy(z + far, e).start()

        @pl.when(jnp.logical_and(z - far >= 0, far > 0))
        def _():
            for e in range(1, PLANE):
                plane_copy(z - far, e).start()

        return 0

    lax.fori_loop(0, LINE, send_out, 0)

    def partial(d):
        for e in range(1, PLANE):
            plane_copy(d, e).wait_recv()
        hit = slot_matrix(pos_ref[d]).astype(jnp.bfloat16)
        terms = got[:, d].reshape(BS, features)
        return lax.dot_general(
            hit, terms, (((0,), (0,)), ((), ())), preferred_element_type=jnp.float32
        )

    def advance(i, _):
        far = LINE - 1 - i
        right, left = z + far, z - far
        go_right, go_left = right < LINE, left >= 0

        @pl.when(go_right)
        def _():
            right_sum[...] = partial(right)

        @pl.when(go_left)
        def _():
            left_sum[...] = partial(left)

        for c in range(PIECES):
            part = piece(c)

            @pl.when(go_right)
            def _():
                @pl.when(z > 0)
                def _():
                    line_copy(right, far + 1, c, 0).wait_recv()
                    right_sum[part, :] += from_left[right, part, :].astype(jnp.float32)

                sums[right, part, :] = right_sum[part, :].astype(jnp.bfloat16)
                line_copy(right, far, c, 0).start()

            @pl.when(go_left)
            def _():
                @pl.when(z < LINE - 1)
                def _():
                    line_copy(left, far + 1, c, 1).wait_recv()
                    left_sum[part, :] += from_right[left, part, :].astype(jnp.float32)

                sums[left, part, :] = left_sum[part, :].astype(jnp.bfloat16)
                line_copy(left, far, c, 1).start()

        return 0

    lax.fori_loop(0, LINE - 1, advance, 0)
    right_sum[...] = partial(z) - act_ref[...].astype(jnp.float32)

    @pl.when(z > 0)
    def _():
        for c in range(PIECES):
            line_copy(z, 1, c, 0).wait_recv()
        right_sum[...] += from_left[z].astype(jnp.float32)

    @pl.when(z < LINE - 1)
    def _():
        for c in range(PIECES):
            line_copy(z, 1, c, 1).wait_recv()
        right_sum[...] += from_right[z].astype(jnp.float32)

    res_ref[...] = right_sum[...].astype(jnp.bfloat16)

    def drain(far, _):
        for c in range(PIECES):
            @pl.when(jnp.logical_and(z + far < LINE, far > 0))
            def _():
                line_copy(z + far, far, c, 0).wait_send()

            @pl.when(jnp.logical_and(z - far >= 0, far > 0))
            def _():
                line_copy(z - far, far, c, 1).wait_send()

        for e in range(1, PLANE):
            plane_copy(far, e).wait_send()
        return 0

    return drain


def column(row):
    r = lax.broadcasted_iota(jnp.int32, (BS, BS), 0)
    col = lax.broadcasted_iota(jnp.int32, (BS, BS), 1)
    return jnp.sum(jnp.where(r == col, row, 0.0), axis=1, keepdims=True)


def flat_row(values):
    r = lax.broadcasted_iota(jnp.int32, (BS, BS), 0)
    col = lax.broadcasted_iota(jnp.int32, (BS, BS), 1)
    return jnp.sum(jnp.where(r == col, values, 0.0), axis=0, keepdims=True)


def step_kernel(x_ref, code_ref, bias_ref, enc_ref, dec_ref,
                enc_grad_ref, grad_ref, bias_grad_ref,
                in_ref, turned_ref, dpre_ref, small_ref, all_a, code_all, stage_a, got_a, line_a, plane_a,
                sq_ref, sq_y, sq_mine, sq_z,
                codes_ref, unit_ref, row_ref, resid_ref, raw_ref, scaled_ref,
                part_b, got_yb, mine_b, got_zb, pre_ref, sems_b,
                terms_ref, res_ref, stage_c, got_c, sums, from_left, from_right, right_sum, left_sum,
                line_c, plane_c,
                all_d, stage_d, got_d, line_d, plane_d,
                part_e, got_ye, mine_e, got_ze, sems_e, pos_ref):
    place = lat_place()
    wid = wid_place()
    hi, y, partner, peers = wid
    features = x_ref.shape[1]
    f32, bf16 = jnp.float32, jnp.bfloat16
    greet(place, wid)

    def sq_copy(d):
        return pltpu.make_async_remote_copy(
            src_ref=sq_ref, dst_ref=sq_y.at[d - 1], send_sem=sems_b.at[0, 13 + d],
            recv_sem=sems_b.at[1, 13 + d], device_id={"wid": peers[d - 1]}, device_id_type=MESH,
        )

    sq_far = pltpu.make_async_remote_copy(
        src_ref=sq_mine, dst_ref=sq_z, send_sem=sems_b.at[0, 17], recv_sem=sems_b.at[1, 17],
        device_id={"wid": partner}, device_id_type=MESH,
    )

    def square():
        for k in range(8):
            wide = dec_ref[k].astype(f32)
            total = jnp.sum(wide * wide, axis=1, keepdims=True)
            sq_ref[k : k + 1, :] = flat_row(total)
        for d in (1, 2, 3):
            sq_copy(d).start()

    def sum_squares():
        for d in (1, 2, 3):
            sq_copy(d).wait()
        sq_mine[...] = sq_ref[...] + sq_y[0] + sq_y[1] + sq_y[2]
        sq_far.start()

    spread(x_ref, all_a, pos_ref, stage_a, got_a, in_ref, line_a, plane_a, place, code_ref, code_all,
           square, sum_squares)

    def partial_preact(h):
        for k in range(4 * h, 4 * h + 4):
            part_b[h, k % 4] = jnp.dot(
                in_ref[k].reshape(BS, features), enc_ref[:, k * BS : (k + 1) * BS],
                preferred_element_type=f32,
            ).astype(bf16)

    def normalize():
        sq_far.wait()
        row_ref[...] = jnp.sqrt(sq_mine[...] + sq_z[...] + EPS)
        for k in range(8):
            norm = column(row_ref[k : k + 1, :])
            unit = (dec_ref[k].astype(f32) / norm).astype(bf16)
            unit_ref[k] = unit
            scaled_ref[k] = unit.astype(f32) / norm

    def live(h):
        return in_ref[h * 4 + y].reshape(BS, features)[:, 0:1].astype(f32) < 1.5

    def encode(h, total):
        preact = total + bias_ref[h * 4 + y]
        pre_ref[h] = preact
        codes_ref[h, y] = jnp.where(live(h), gelu(preact), 0.0).astype(bf16)
        return hand_on(codes_ref.at[h, y], sems_b, 7 + 3 * h, wid)

    wid_sum(part_b, got_yb, mine_b, got_zb, sems_b, wid, partial_preact, normalize, encode)

    for k in range(8):
        terms_ref[k] = (
            jnp.dot(codes_ref[k // 4, k % 4], unit_ref[k], preferred_element_type=f32)
            .astype(bf16)
            .reshape(PLANE, 16, features)
        )
    drain = collect(terms_ref, x_ref, pos_ref, res_ref, stage_c, got_c, sums, from_left,
                    from_right, right_sum, left_sum, line_c, plane_c, place)
    spread(res_ref, all_d, pos_ref, stage_d, got_d, resid_ref, line_d, plane_d, place)

    def partial_dcode(h):
        for k in range(4 * h, 4 * h + 4):
            part_e[h, k % 4] = lax.dot_general(
                resid_ref[k].reshape(BS, features), unit_ref[k], (((1,), (1,)), ((), ())),
                preferred_element_type=f32,
            ).astype(bf16)

    def decoder_sums():
        for k in range(8):
            raw = lax.dot_general(
                codes_ref[k // 4, k % 4], resid_ref[k].reshape(BS, features), (((0,), (0,)), ((), ())),
                preferred_element_type=f32,
            )
            raw_ref[k] = raw / column(row_ref[k : k + 1, :])
            turned_ref[k] = in_ref[k].reshape(BS, features).T
        lax.fori_loop(0, LINE, drain, 0)

    def differentiate(h, dcode):
        dpre = jnp.where(live(h), dcode * gelu_slope(pre_ref[h]), 0.0)
        dpre_ref[h, y] = dpre.astype(bf16)
        along = jnp.sum(codes_ref[h, y].astype(f32) * dcode, axis=0, keepdims=True)
        bias_grad = jnp.sum(dpre, axis=0, keepdims=True)
        row = lax.broadcasted_iota(jnp.int32, (8, BS), 0)
        small_ref[h, y] = jnp.where(row == 0, along, bias_grad)
        return hand_on(dpre_ref.at[h, y], sems_e, 7 + 3 * h, wid) + hand_on(
            small_ref.at[h, y], sems_e, 13 + 3 * h, wid
        )

    wid_sum(part_e, got_ye, mine_e, got_ze, sems_e, wid, partial_dcode, decoder_sums, differentiate)
    for k in range(8):
        enc_grad_ref[:, k * BS : (k + 1) * BS] = jnp.dot(
            turned_ref[k], dpre_ref[k // 4, k % 4], preferred_element_type=f32
        ).astype(bf16)
        bias_grad_ref[k : k + 1, :] = small_ref[k // 4, k % 4, 1:2, :]
        along = column(small_ref[k // 4, k % 4, 0:1, :])
        grad_ref[k] = (raw_ref[k] - along * scaled_ref[k]).astype(bf16)


def slots_buffer(features):
    return pltpu.VMEM((8, 8, 16, features), jnp.bfloat16)


def lat_sems():
    return [pltpu.SemaphoreType.DMA((2, 2, LINE, PIECES + 1)), pltpu.SemaphoreType.DMA((2, LINE, PLANE - 1))]


def run_step(x, codes, bias, encoder, decoder):
    rows, features = BS, x.shape[1]
    f32, bf16 = jnp.float32, jnp.bfloat16
    slots = 2 * LINE * PLANE
    row_blocks = pltpu.VMEM((LINE, rows, features), bf16)
    slot = slots_buffer(features)
    wid_part = pltpu.VMEM((2, 4, slots, BS), bf16)
    sq_block = pltpu.VMEM((8, BS), f32)
    row_total = pltpu.VMEM((rows, features), f32)
    latents = pltpu.VMEM((8, BS, features), f32)
    return pl.pallas_call(
        step_kernel,
        out_shape=(
            jax.ShapeDtypeStruct((features, 8 * BS), bf16),
            jax.ShapeDtypeStruct((8, BS, features), bf16),
            jax.ShapeDtypeStruct((8, BS), f32),
        ),
        in_specs=vmem(5),
        out_specs=tuple(vmem(3)),
        scratch_shapes=[slot, pltpu.VMEM((8, features, BS), bf16), wid_part]
        + [pltpu.VMEM((2, 4, 8, BS), f32)]
        + [row_blocks, pltpu.VMEM((LINE, 16, BS), bf16), slot, slot]
        + lat_sems()
        + [sq_block, pltpu.VMEM((3, 8, BS), f32), sq_block, sq_block]
        + [wid_part, pltpu.VMEM((8, BS, features), bf16), sq_block, slot, latents, latents]
        + [wid_part]
        + sum_scratch(slots)
        + [pltpu.VMEM((2, slots, BS), f32), pltpu.SemaphoreType.DMA((2, 18))]
        + [slot, pltpu.VMEM((rows, features), bf16), slot, slot]
        + [row_blocks, row_blocks, row_blocks, row_total, row_total]
        + lat_sems()
        + [row_blocks, slot, slot]
        + lat_sems()
        + [wid_part]
        + sum_scratch(slots)
        + [pltpu.SemaphoreType.DMA((2, 20)), pltpu.VMEM((LINE, 8, BS), f32)],
        compiler_params=pltpu.CompilerParams(collective_id=0, has_side_effects=True),
        name="step",
    )(x, codes, bias, encoder, decoder)


def body(activations, block_ids, alive_tallies, encoder, encoder_bias, decoder):
    rows, features = activations.shape
    slots = block_ids.shape[1]
    lat = lax.axis_size("lat")
    f32 = jnp.float32

    flat = block_ids.reshape(rows * slots)
    order = jnp.arange(rows * slots, dtype=jnp.int32)
    earlier = (flat[:, None] == flat[None, :]) & (order[None, :] < order[:, None])
    rank = jnp.sum(earlier.astype(jnp.int32), axis=1).reshape(rows, slots)
    alive = jnp.arange(slots, dtype=jnp.int32)[None, :] < alive_tallies[:, None]
    position = block_ids * 2 + rank
    high = jnp.where(alive, position >> 3, 255)
    codes_of_rows = jnp.concatenate([high, position & 7], axis=1).T.astype(jnp.bfloat16)
    extra = jnp.pad(codes_of_rows, ((0, 8), (0, 0)))
    encoder_grad, decoder_grad, bias_grad = run_step(
        activations, extra, encoder_bias.reshape(8, 1, BS), encoder, decoder.reshape(8, BS, features)
    )
    decoder_grad = decoder_grad.reshape(8 * BS, features)
    bias_grad = bias_grad.reshape(8 * BS)
    return encoder_grad, decoder_grad, bias_grad


def solution(mesh):
    return jax.shard_map(
        body,
        mesh=mesh,
        in_specs=(
            P("lat", "wid"),
            P("lat", None),
            P("lat"),
            P("wid", "lat"),
            P("lat"),
            P("lat", "wid"),
        ),
        out_specs=(P("wid", "lat"), P("lat", "wid"), P("lat")),
        check_vma=False,
    )
```
